128 devices in a mesh: seq: 16 (over x_hi, y, core), chan: 8 (over z, x_lo).
Axes of the slice: x: 4 (x_hi: 2, x_lo: 2; x = x_hi * 2 + x_lo), y: 4, z: 4, core: 2. Of those that a mesh axis runs over, the one named last changes fastest.
Arguments:
- out_grad: bfloat16 [8192, 8192], P('seq', 'chan'), may hold values from -6 to 6
- out_weight: bfloat16 [1024, 8192], P(None, 'chan'), may hold values from -0.0625 to 0.0625
- conv_input: bfloat16 [1024, 8192], P('chan', 'seq'), may hold values from -6 to 6
- gate_values: bfloat16 [1024, 8192], P('chan', 'seq'), may hold values from -6 to 6
- conv_output: bfloat16 [1024, 8192], P('chan', 'seq'), may hold values from -6 to 6
- filters: bfloat16 [2, 1024, 512], P(None, 'chan'), may hold values from -0.29882812 to 0.29882812
- filter_reach: int32 [16], replicated, may hold values from 128 to 512, as said below
Outputs:
- grad_input: float32 [1024, 8192], P('chan', 'seq')
- grad_gate: float32 [1024, 8192], P('chan', 'seq')
- grad_weight: float32 [1024, 8192], P('seq', 'chan')
- grad_filters: float32 [2, 1024, 512], P(None, 'chan', 'seq')
The draws below stay inside these ranges and needn't reach their ends.
Inputs may be any that keep to these rules, and one draw needn't show every extreme that they name: `filter_reach`: group g holds channels g * 64 to (g + 1) * 64 - 1. Every reach is a multiple of 128, and at least one group has reach 512.
All inputs are finite; a program needn't handle non-finite values.
Results may differ from the reference program's by a relative error of at most 0.014.
Values may be sent and summed in bfloat16 or wider, within the bound.
No kernel may reach another device: no remote copies, remote signals or barrier semaphores. Data moves between devices by JAX's collectives and lax.ppermute only.
A program may use at most 128 MiB of HBM per device.

```python
import jax
import jax.numpy as jnp
from jax import lax

D = 8192
C = 1024
GROUP = 64
TAPS = 512
TOKENS = 8192
N_CHAN = 8


def draw_filter_reach(key, part):
    levels = TAPS // 128
    groups_total = C // GROUP
    key_multiples, second = jax.random.split(jax.random.fold_in(key, 17))
    multiples = jax.random.randint(key_multiples, (groups_total,), 1, levels + 1)
    chosen = jax.random.randint(second, (), 0, groups_total)
    picked = jnp.where(jnp.arange(groups_total) == chosen, levels, multiples)
    return (128 * picked).astype(jnp.int32)


def block_levels(own_key, dims, pieces, low, largest):
    factor_of, own = 1.0, jax.random.fold_in(own_key, 6)
    for axis_at, parts in pieces:
        heights = jnp.exp(jax.random.uniform(jax.random.fold_in(own, axis_at), (parts,), jnp.float32, low / len(pieces), largest / len(pieces)))
        factor_of = factor_of * jnp.repeat(heights, dims[axis_at] // parts).reshape([-1 if axis == axis_at else 1 for axis in range(len(dims))])
    return factor_of


def scatter_about(own_key, shape, scale, limit, pieces=(), held_as=jnp.bfloat16):
    entries = scale * jax.random.normal(own_key, shape, jnp.float32)
    if pieces:
        entries = entries * block_levels(own_key, shape, pieces, -0.22, 0.18)
    return jnp.clip(entries, -limit, limit).astype(held_as)


def setup_inputs(seed: int = 0) -> dict:
    key_list = jax.random.split(jax.random.key(seed), 8)
    out_grad = scatter_about(key_list[0], (TOKENS, D), 1.0, 6.0, ((0, 16), (1, 8)))
    out_weight = scatter_about(key_list[1], (C, D), D ** -0.5, 0.0625, ((1, 8),))
    conv_input = scatter_about(key_list[2], (C, TOKENS), 1.0, 6.0, ((0, 8), (1, 16)))
    gate_values = scatter_about(key_list[3], (C, TOKENS), 1.0, 6.0, ((0, 8), (1, 16)))
    conv_output = scatter_about(key_list[4], (C, TOKENS), 1.0, 6.0, ((0, 8), (1, 16)))
    filters = scatter_about(key_list[5], (2, C, TAPS), 0.05, 0.29882812, ((1, 8),))
    filter_reach = draw_filter_reach(jax.random.fold_in(key_list[7], 71), 0)
    return {"out_grad": out_grad, "out_weight": out_weight, "conv_input": conv_input, "gate_values": gate_values, "conv_output": conv_output, "filters": filters, "filter_reach": filter_reach}


def reference(out_grad, out_weight, conv_input, gate_values, conv_output, filters, filter_reach):
    feature_block = D // N_CHAN
    grad_gated = jnp.zeros((C, TOKENS), jnp.float32)
    for portion in range(N_CHAN):
        weight_cols = out_weight[:, portion * feature_block:(portion + 1) * feature_block]
        grad_cols = out_grad[:, portion * feature_block:(portion + 1) * feature_block]
        partial_value = jnp.dot(weight_cols, grad_cols.T, preferred_element_type=jnp.float32)
        rounded = lax.optimization_barrier(partial_value.astype(jnp.bfloat16))
        grad_gated = grad_gated + rounded.astype(jnp.float32)
    grad_scale = 1.0 / (TOKENS ** 0.5)
    gated = (conv_output.astype(jnp.float32) * gate_values.astype(jnp.float32)).astype(jnp.bfloat16)
    grad_weight = jnp.dot(gated, out_grad, preferred_element_type=jnp.float32) * grad_scale
    grad_gate = grad_gated * conv_output.astype(jnp.float32)
    grad_conv = (grad_gated * gate_values.astype(jnp.float32)).astype(jnp.bfloat16)
    channel_reach = filter_reach[jnp.arange(C, dtype=jnp.int32) // GROUP]
    inside = jnp.arange(TAPS, dtype=jnp.int32)[None, :] < channel_reach[:, None]
    forward_taps = jnp.where(inside, filters[0], jnp.zeros((), filters.dtype)).astype(jnp.float32)
    backward_taps = jnp.where(inside, filters[1], jnp.zeros((), filters.dtype)).astype(jnp.float32)
    shifted_back = jnp.pad(backward_taps, ((0, 0), (1, 0)))
    fft_len = TOKENS + 2 * TAPS
    grad_spec = jnp.fft.rfft(grad_conv.astype(jnp.float32), n=fft_len, axis=1)
    input_spec = jnp.fft.rfft(conv_input.astype(jnp.float32), n=fft_len, axis=1)
    ahead_spec = jnp.fft.rfft(forward_taps, n=fft_len, axis=1)
    behind_spec = jnp.fft.rfft(shifted_back, n=fft_len, axis=1)
    grad_input = jnp.fft.irfft(grad_spec * jnp.conj(ahead_spec), n=fft_len, axis=1)[:, :TOKENS]
    grad_input = grad_input + jnp.fft.irfft(grad_spec * behind_spec, n=fft_len, axis=1)[:, :TOKENS]
    ahead_grad = jnp.fft.irfft(grad_spec * jnp.conj(input_spec), n=fft_len, axis=1)[:, :TAPS]
    behind_grad = jnp.fft.irfft(jnp.conj(grad_spec) * input_spec, n=fft_len, axis=1)[:, 1:TAPS + 1]
    grad_filters = jnp.stack([ahead_grad, behind_grad]) * inside[None].astype(ahead_grad.dtype) * grad_scale
    return grad_input, grad_gate, grad_weight, grad_filters
```

```python
import jax
import jax.numpy as jnp
from jax import lax
from jax.experimental import pallas as pl
from jax.experimental.pallas import tpu as pltpu
from jax.sharding import PartitionSpec as P

GROUP = 64
VN = 32
F32 = jnp.float32
BF16 = jnp.bfloat16


def iota(shape, dim):
    return lax.broadcasted_iota(jnp.int32, shape, dim)


def dot(a, b, dims=(((1,), (0,)), ((), ()))):
    return lax.dot_general(a, b, dims, preferred_element_type=F32)


NT = (((1,), (1,)), ((), ()))


def first_product(pos_ref, w_ref, og_ref, s0, k0, s1, k1):
    z = pos_ref[0]
    x = pos_ref[1]
    half = og_ref.shape[0] // 2
    plan = (
        (0, ((k0, 0, 0), (s0, 0, 1), (k0, 1, 3), (s0, 1, 2))),
        (1, ((k1, 0, 0), (s1, 0, 3), (k1, 1, 1), (s1, 1, 2))),
    )
    for h, items in plan:
        og = og_ref[h * half : (h + 1) * half, :]
        for ref, slot, rel in items:
            for a in range(2):
                row = ((z ^ rel) * 2 + (x ^ a)) * 128
                w = w_ref[pl.ds(row, 128), :]
                ref[slot, 128 * a : 128 * (a + 1), :] = dot(w, og, NT).astype(BF16)


def second_kernel(pos_ref, own, rx, a1, b1, a2, b2, og_ref, ogs_ref, s0, k0, s1, k1, g_ref):
    g_ref[0] = own[...]
    g_ref[1] = a1[...]
    g_ref[3] = a2[0]
    g_ref[2] = a2[1]
    g_ref[4] = rx[...]
    g_ref[7] = b1[...]
    g_ref[5] = b2[0]
    g_ref[6] = b2[1]
    z = pos_ref[0]
    x = pos_ref[1]
    xh = pos_ref[2]
    y = pos_ref[3]
    tok = og_ref.shape[0]
    plan = (
        ((k0, 0, 0, 0), (s0, 0, 0, 1), (k0, 1, 0, 3), (s0, 1, 0, 2)),
        ((k1, 0, 1, 0), (s1, 0, 1, 3), (k1, 1, 1, 1), (s1, 1, 1, 2)),
    )
    for items in plan:
        for ref, slot, xr, yr in items:
            j = (xh ^ xr) * 4 + (y ^ yr)
            jz = j // 2
            jx = j % 2
            src = (jx ^ x) * 4 + (jz ^ z)
            g = g_ref[src]
            ref[slot] = (dot(g[:, :tok], og_ref[...]) + dot(g[:, tok:], ogs_ref[...])).astype(BF16)


def input_grad_kernel(gl_ref, gm_ref, gr_ref, f_ref, o_ref, h_ref):
    n = gm_ref.shape[1]
    width = 3 * n
    own_rows = iota((128, 256), 0) % 8 == iota((128, 256), 1) % 8
    ef = (iota((128, 256), 0) == iota((128, 256), 1) // 8).astype(BF16)
    eb = (iota((128, 256), 0) == (VN - 1) - iota((128, 256), 1) // 8).astype(BF16)
    ext16 = jnp.concatenate([gl_ref[...], gm_ref[...], gr_ref[...]], axis=1).astype(F32)
    filt16 = f_ref[...].astype(F32)
    for h in range(2):
        ext = ext16[8 * h : 8 * h + 8]
        for k in range(VN // 2):
            pair = [ext if v == 0 else pltpu.roll(ext, width - v, 1) for v in (2 * k, 2 * k + 1)]
            h_ref[h, 16 * k : 16 * k + 16, :] = jnp.concatenate(pair, axis=0).astype(BF16)
        lhs = []
        for d, e in ((0, ef), (1, eb)):
            f8 = filt16[d, 8 * h : 8 * h + 8]
            taps = f8.shape[1]
            rolled = [f8 if b == 0 else pltpu.roll(f8, taps - 32 * b, 1) for b in range(4)]
            rows = [rolled[u % 4][:, 128 * (u // 4) : 128 * (u // 4) + 128] for u in range(16)]
            spread = dot(jnp.concatenate(rows, axis=0).astype(BF16), e)
            lhs.append(jnp.where(own_rows, spread, 0.0).astype(BF16))
        pf = dot(lhs[0], h_ref[h, :, n : 3 * n])
        pb = dot(lhs[1], h_ref[h, :, 0 : 2 * n])
        total = None
        for b in range(4):
            acc = None
            for a in range(4):
                u = 4 * a + b
                part = pf[8 * u : 8 * u + 8, 128 * a : 128 * a + n + 128]
                acc = part if acc is None else acc + part
            if b:
                acc = pltpu.roll(acc, n + 128 - 32 * b, 1)
            acc = acc[:, :n]
            total = acc if total is None else total + acc
        for b in range(4):
            acc = None
            for a in range(1, 5) if b == 0 else range(4):
                u = 4 * a + b - 1
                start = n - 128 - 128 * a
                if b == 0:
                    part = pb[8 * u : 8 * u + 8, start + 128 : start + 128 + n]
                else:
                    part = pb[8 * u : 8 * u + 8, start : start + n + 128]
                acc = part if acc is None else acc + part
            if b:
                acc = pltpu.roll(acc, 32 * b, 1)[:, 128:]
            total = total + acc
        o_ref[8 * h : 8 * h + 8, :] = total


def tap_grad_kernel(pos_ref, gm_ref, xl_ref, xm_ref, xr_ref, keep_ref, send_ref, h_ref, u_ref):
    n = gm_ref.shape[1]
    width = 3 * n
    step = pl.program_id(0)
    place = pos_ref[4]
    own_cols = iota((16, 8, 256), 1) == iota((16, 8, 256), 2) % 8
    ext16 = jnp.concatenate([xl_ref[...], xm_ref[...], xr_ref[...]], axis=1).astype(F32)
    zero = jnp.zeros((8, n), F32)
    own16 = gm_ref[...].astype(F32)
    for h in range(2):
        ext = ext16[8 * h : 8 * h + 8]
        for k in range(VN // 2):
            pair = [ext if v == 0 else pltpu.roll(ext, v, 1) for v in (2 * k, 2 * k + 1)]
            h_ref[h, 16 * k : 16 * k + 16, :] = jnp.concatenate(pair, axis=0).astype(BF16)
        own = jnp.concatenate([zero, own16[8 * h : 8 * h + 8], zero], axis=1)
        ahead = [own if b == 0 else pltpu.roll(own, width - 32 * b, 1) for b in range(4)]
        behind = [own if b == 0 else pltpu.roll(own, 32 * b, 1) for b in range(4)]
        for d in range(2):
            for k in range(8):
                pair = []
                for u in (2 * k, 2 * k + 1):
                    if d == 0:
                        start = 128 * (u // 4)
                        pair.append(ahead[u % 4][:, start : start + 2 * n])
                    else:
                        start = n - 128 * ((u + 1) // 4)
                        pair.append(behind[(u + 1) % 4][:, start : start + 2 * n])
                u_ref[h, d, 16 * k : 16 * k + 16, :] = jnp.concatenate(pair, axis=0).astype(BF16)
        for d in range(2):
            cross = dot(u_ref[h, d], h_ref[h, :, n * d : n * d + 2 * n], NT)
            sums = jnp.sum(jnp.where(own_cols, cross.reshape(16, 8, 256), 0.0), axis=1)
            row = d * (keep_ref.shape[1] // 2) + 2 * step + h
            for u in range(16):
                r = u ^ place
                line = sums[u : u + 1]

                @pl.when(r % 2 == 0)
                def _():
                    keep_ref[r // 2, pl.ds(row, 1), :] = line

                @pl.when(r % 2 == 1)
                def _():
                    send_ref[r // 2, pl.ds(row, 1), :] = line


def finish_taps_kernel(s_ref, m_ref, o_ref):
    ef = (iota((256, VN), 1) == iota((256, VN), 0) // 8).astype(F32)
    eb = (iota((256, VN), 1) == (VN - 1) - iota((256, VN), 0) // 8).astype(F32)
    own_cols = iota((16, 8, 256), 1) == iota((16, 8, 256), 2) % 8
    for d, e in ((0, ef), (1, eb)):
        s = s_ref[16 * d : 16 * d + 16, :]
        wide = jnp.broadcast_to(s[:, None, :], (16, 8, 256))
        wide = jnp.where(own_cols, wide, 0.0).reshape(128, 256)
        taps = lax.dot_general(
            wide, e, (((1,), (0,)), ((), ())),
            precision=lax.Precision.HIGHEST, preferred_element_type=F32,
        )
        o_ref[d] = taps * m_ref[...]


def xor_of(count, mask):
    return [(i, i ^ mask) for i in range(count)]


def seq_swap(v, mask):
    return lax.ppermute(v, "seq", xor_of(lax.axis_size("seq"), mask))


def chan_swap(v, mask):
    return lax.ppermute(v, "chan", xor_of(lax.axis_size("chan"), mask))


def add16(a, b):
    return (a.astype(F32) + b.astype(F32)).astype(BF16)


def smem():
    return pl.BlockSpec(memory_space=pltpu.SMEM)


def on_device(out_grad, out_weight, conv_input, gate_values, conv_output, filters, filter_reach):
    rows, tok = conv_input.shape
    taps = filters.shape[2]
    feats = out_grad.shape[1]
    seq_count = lax.axis_size("seq")
    place = lax.axis_index("seq").astype(jnp.int32)
    chan = lax.axis_index("chan").astype(jnp.int32)
    core = place % 2
    pos = jnp.stack([chan // 2, chan % 2, place // 8, (place // 2) % 4, place])
    vmem = pl.BlockSpec(memory_space=pltpu.VMEM)
    shift_up = [(i, i + 1) for i in range(seq_count - 1)]
    shift_down = [(i + 1, i) for i in range(seq_count - 1)]
    half = rows // 2

    gated = (conv_output.astype(F32) * gate_values.astype(F32)).astype(BF16)
    mine = lax.dynamic_slice_in_dim(gated, core * half, half, 0)
    other = lax.dynamic_slice_in_dim(gated, (1 - core) * half, half, 0)
    from_core = seq_swap(other, 1)
    grad_core = seq_swap(out_grad, 1)
    own = jnp.concatenate([mine, from_core], axis=1)
    rx = chan_swap(own, 1)
    a1 = chan_swap(own, 2)
    b1 = chan_swap(rx, 6)
    a2 = chan_swap(jnp.stack([own, a1]), 6)
    b2 = chan_swap(jnp.stack([rx, b1]), 2)

    piece = jax.ShapeDtypeStruct((2, 256, tok // 2), BF16)
    s0, k0, s1, k1 = pl.pallas_call(
        first_product,
        out_shape=[piece] * 4,
        in_specs=[smem(), vmem, vmem],
        out_specs=[vmem] * 4,
        name="first_product",
    )(pos, out_weight, out_grad)
    r0 = chan_swap(s0, 2)
    r1 = chan_swap(s1, 6)
    q0 = chan_swap(add16(k0[1], r0[1]), 6)
    q1 = chan_swap(add16(k1[1], r1[1]), 2)
    t0 = k0[0].astype(F32) + r0[0].astype(F32) + q0.astype(F32)
    t1 = k1[0].astype(F32) + r1[0].astype(F32) + q1.astype(F32)
    away = jnp.concatenate([t0[128:], t1[128:]], axis=1).astype(BF16)
    grad_gated = jnp.concatenate([t0[:128], t1[:128]], axis=1) + chan_swap(away, 1).astype(F32)
    grad_gate = grad_gated * conv_output.astype(F32)
    grad_conv = (grad_gated * gate_values.astype(F32)).astype(BF16)

    xl = lax.ppermute(conv_input, "seq", shift_up)
    xr = lax.ppermute(conv_input, "seq", shift_down)
    gl = lax.ppermute(grad_conv, "seq", shift_up)
    gr = lax.ppermute(grad_conv, "seq", shift_down)

    piece = jax.ShapeDtypeStruct((2, half, feats), BF16)
    e_s0, e_k0, e_s1, e_k1 = pl.pallas_call(
        second_kernel,
        out_shape=[piece] * 4,
        in_specs=[smem()] + [vmem] * 8,
        out_specs=[vmem] * 4,
        scratch_shapes=[pltpu.VMEM((8, half, 2 * tok), BF16)],
        name="second_product",
    )(pos, own, rx, a1, b1, a2, b2, out_grad, grad_core)
    e_r0 = seq_swap(e_s0, 2)
    e_r1 = seq_swap(e_s1, 6)
    e_q0 = seq_swap(add16(e_k0[1], e_r0[1]), 6)
    e_q1 = seq_swap(add16(e_k1[1], e_r1[1]), 2)
    e_t1 = (e_k1[0].astype(F32) + e_r1[0].astype(F32) + e_q1.astype(F32)).astype(BF16)
    e_x = seq_swap(e_t1, 8)
    scale = 1.0 / float(tok * seq_count) ** 0.5
    grad_weight = (
        e_k0[0].astype(F32) + e_r0[0].astype(F32) + e_q0.astype(F32) + e_x.astype(F32)
    ) * scale

    ids = (chan * rows + jnp.arange(rows, dtype=jnp.int32)) // GROUP
    levels = jnp.arange(filter_reach.shape[0], dtype=jnp.int32)
    reach = jnp.sum(jnp.where(ids[:, None] == levels[None, :], filter_reach[None, :], 0), axis=1)
    inside = jnp.arange(taps, dtype=jnp.int32)[None, :] < reach[:, None]
    masked = jnp.where(inside[None], filters, jnp.zeros((), filters.dtype))

    band = pl.BlockSpec((16, tok), lambda g: (g, 0))
    lag_out = jax.ShapeDtypeStruct((8, rows // 4, 256), F32)
    whole = pl.BlockSpec((8, rows // 4, 256), lambda g: (0, 0, 0))
    f_keep, f_send = pl.pallas_call(
        tap_grad_kernel,
        grid=(rows // 16,),
        out_shape=[lag_out] * 2,
        in_specs=[smem(), band, band, band, band],
        out_specs=[whole] * 2,
        scratch_shapes=[
            pltpu.VMEM((2, 256, 3 * tok), BF16),
            pltpu.VMEM((2, 2, 128, 2 * tok), BF16),
        ],
        name="tap_grad",
    )(pos, grad_conv, xl, conv_input, xr)
    f1 = f_keep + seq_swap(f_send.astype(BF16), 1).astype(F32)
    f1 = f1.reshape((2, 4) + f1.shape[1:])
    first = jnp.stack([f1[:, 1], f1[:, 2]]).astype(BF16)
    f2 = jnp.stack([f1[:, 0], f1[:, 3]]) + seq_swap(first, 2).astype(F32)
    f3 = f2[0] + seq_swap(f2[1].astype(BF16), 6).astype(F32)
    f4 = f3[0] + seq_swap(f3[1].astype(BF16), 8).astype(F32)
    lag = place * VN + jnp.arange(VN, dtype=jnp.int32)
    lag_mask = (lag[None, :] < reach[:, None]).astype(F32) * scale
    grad_filters = pl.pallas_call(
        finish_taps_kernel,
        out_shape=jax.ShapeDtypeStruct((2, rows, VN), F32),
        in_specs=[vmem, vmem],
        out_specs=vmem,
        name="finish_taps",
    )(f4, lag_mask)

    grad_input = pl.pallas_call(
        input_grad_kernel,
        grid=(rows // 16,),
        out_shape=jax.ShapeDtypeStruct((rows, tok), F32),
        in_specs=[band, band, band, pl.BlockSpec((2, 16, taps), lambda g: (0, g, 0))],
        out_specs=band,
        scratch_shapes=[pltpu.VMEM((2, 256, 3 * tok), BF16)],
        name="input_grad",
    )(gl, grad_conv, gr, masked)
    return (grad_input, grad_gate, grad_weight, grad_filters)


def solution(mesh):
    return jax.shard_map(
        on_device,
        mesh=mesh,
        in_specs=(
            P("seq", "chan"),
            P(None, "chan"),
            P("chan", "seq"),
            P("chan", "seq"),
            P("chan", "seq"),
            P(None, "chan", None),
            P(),
        ),
        out_specs=(P("chan", "seq"), P("chan", "seq"), P("seq", "chan"), P(None, "chan", "seq")),
        check_vma=False,
    )
```

```python
import functools

import jax
import jax.numpy as jnp
from jax import lax
from jax.experimental import pallas as pl
from jax.experimental.pallas import tpu as pltpu
from jax.sharding import PartitionSpec as P


GROUP = 64
VN = 32
F32 = jnp.float32
BF16 = jnp.bfloat16


def iota(shape, dim):
    return lax.broadcasted_iota(jnp.int32, shape, dim)


def dot(a, b, dims=(((1,), (0,)), ((), ()))):
    return lax.dot_general(a, b, dims, preferred_element_type=F32)


NT = (((1,), (1,)), ((), ()))


RELS = (0, 1, 3, 2)


def gate_rows(pos_ref, v_ref, g_ref, mine, other):
    half = mine.shape[0]
    core = pos_ref[4] % 2
    for ref, part in ((mine, core), (other, 1 - core)):
        band = pl.ds(pl.multiple_of(part * half, half), half)
        ref[...] = (v_ref[band, :].astype(F32) * g_ref[band, :].astype(F32)).astype(BF16)


def first_product(pos_ref, w_ref, og_ref, *outs):
    z = pos_ref[0]
    x = pos_ref[1]
    og = og_ref[...]
    for ref, rel in zip(outs, RELS):
        for a in range(2):
            row = ((z ^ rel) * 2 + (x ^ a)) * 128
            ref[128 * a : 128 * (a + 1), :] = dot(w_ref[pl.ds(row, 128), :], og, NT).astype(BF16)


def second_product(pos_ref, b0, b1, b3, b2, bx, og_ref, ogs_ref, *refs):
    outs, g_ref = refs[:4], refs[4]
    for i, ref in enumerate((b0, b1, b2, b3)):
        g_ref[i] = ref[...]
        g_ref[4 + i] = bx[i]
    z = pos_ref[0]
    x = pos_ref[1]
    xh = pos_ref[2]
    y = pos_ref[3]
    tok = og_ref.shape[0]
    for ref, rel in zip(outs, RELS):
        for a in range(2):
            j = (xh ^ a) * 4 + (y ^ rel)
            g = g_ref[((j % 2) ^ x) * 4 + ((j // 2) ^ z)]
            ref[a] = (dot(g[:, :tok], og_ref[...]) + dot(g[:, tok:], ogs_ref[...])).astype(BF16)


def conv_grads(pos_ref, reach_ref, gm_ref, gs_ref, gp_ref, f_ref, x_ref, o_ref, t_ref, h_ref, u_ref):
    rows, n = gm_ref.shape
    width = 3 * n
    chan = pos_ref[0] * 2 + pos_ref[1]
    place = pos_ref[4]
    core0 = place % 2 == 0
    own_rows = iota((128, 256), 0) % 8 == iota((128, 256), 1) % 8
    own_cols = iota((16, 8, 256), 1) == iota((16, 8, 256), 2) % 8
    ef = (iota((128, 256), 0) == iota((128, 256), 1) // 8).astype(BF16)
    eb = (iota((128, 256), 0) == (VN - 1) - iota((128, 256), 1) // 8).astype(BF16)
    taps = f_ref.shape[2]
    lag = iota((8, taps), 1)

    def step(i, carry):
        base = pl.multiple_of(i * 16, 16)
        band = pl.ds(base, 16)
        gm = gm_ref[band, :].astype(F32)
        gs = gs_ref[band, :].astype(F32)
        gp = gp_ref[band, :].astype(F32)
        gl = jnp.where(core0, gp, gs)
        gr = jnp.where(core0, gs, gp)
        ext16 = jnp.concatenate([gl, gm, gr], axis=1)
        own16 = x_ref[band, :].astype(F32)
        filt16 = [f_ref[d, band, :].astype(F32) for d in range(2)]
        inside = lag < reach_ref[(chan * rows + base) // GROUP]
        zero = jnp.zeros((8, n), F32)
        outs = []
        for h in range(2):
            ext = ext16[8 * h : 8 * h + 8]
            for k in range(VN // 2):
                pair = [ext if v == 0 else pltpu.roll(ext, width - v, 1) for v in (2 * k, 2 * k + 1)]
                h_ref[h, 16 * k : 16 * k + 16, :] = jnp.concatenate(pair, axis=0).astype(BF16)
            lhs = []
            for d, e in ((0, ef), (1, eb)):
                f8 = jnp.where(inside, filt16[d][8 * h : 8 * h + 8], 0.0)
                rolled = [f8 if b == 0 else pltpu.roll(f8, taps - 32 * b, 1) for b in range(4)]
                cut = [rolled[u % 4][:, 128 * (u // 4) : 128 * (u // 4) + 128] for u in range(16)]
                spread = dot(jnp.concatenate(cut, axis=0).astype(BF16), e)
                lhs.append(jnp.where(own_rows, spread, 0.0).astype(BF16))
            pf = dot(lhs[0], h_ref[h, :, n : 3 * n])
            pb = dot(lhs[1], h_ref[h, :, 0 : 2 * n])
            total = None
            for b in range(4):
                acc = None
                for a in range(4):
                    u = 4 * a + b
                    part = pf[8 * u : 8 * u + 8, 128 * a : 128 * a + n + 128]
                    acc = part if acc is None else acc + part
                if b:
                    acc = pltpu.roll(acc, n + 128 - 32 * b, 1)
                acc = acc[:, :n]
                total = acc if total is None else total + acc
            for b in range(4):
                acc = None
                for a in range(1, 5) if b == 0 else range(4):
                    u = 4 * a + b - 1
                    start = n - 128 - 128 * a
                    if b == 0:
                        part = pb[8 * u : 8 * u + 8, start + 128 : start + 128 + n]
                    else:
                        part = pb[8 * u : 8 * u + 8, start : start + n + 128]
                    acc = part if acc is None else acc + part
                if b:
                    acc = pltpu.roll(acc, 32 * b, 1)[:, 128:]
                total = total + acc
            outs.append(total)
            own = jnp.concatenate([zero, own16[8 * h : 8 * h + 8], zero], axis=1)
            later = [own if b == 0 else pltpu.roll(own, 32 * b, 1) for b in range(4)]
            sooner = [own if b == 0 else pltpu.roll(own, width - 32 * b, 1) for b in range(4)]
            for d in range(2):
                for k in range(8):
                    pair = []
                    for u in (2 * k, 2 * k + 1):
                        if d == 0:
                            start = n - 128 * (u // 4)
                            pair.append(later[u % 4][:, start : start + 2 * n])
                        else:
                            start = 128 * ((u + 1) // 4)
                            pair.append(sooner[(u + 1) % 4][:, start : start + 2 * n])
                    u_ref[h, d, 16 * k : 16 * k + 16, :] = jnp.concatenate(pair, axis=0).astype(BF16)
            for d in range(2):
                start = n * (1 - d)
                cross = dot(u_ref[h, d], h_ref[h, :, start : start + 2 * n], NT)
                sums = jnp.sum(jnp.where(own_cols, cross.reshape(16, 8, 256), 0.0), axis=1)
                row = d * (rows // 8) + 2 * i + h
                for u in range(16):
                    r = u ^ place
                    slot = (r % 2) * 8 + ((r // 2) % 4) * 2 + r // 8
                    t_ref[slot, pl.ds(row, 1), :] = sums[u : u + 1]
        o_ref[band, :] = jnp.concatenate(outs, axis=0)
        return carry

    lax.fori_loop(0, rows // 16, step, 0)


def split_taps(t_ref, got_ref, k, s1, s3, s2):
    for rel, ref in ((0, k), (1, s1), (3, s3), (2, s2)):
        both = t_ref[2 * rel : 2 * rel + 2] + got_ref[2 * rel : 2 * rel + 2].astype(F32)
        ref[...] = both.astype(ref.dtype)


def last_send(ek, e1, e3, e2, fk, f1, f3, f2, o_ref):
    e = ek[1].astype(F32)
    for ref in (e1, e3, e2):
        e = e + ref[1].astype(F32)
    f = fk[1]
    for ref in (f1, f3, f2):
        f = f + ref[1].astype(F32)
    n = f.shape[0] // 4
    o_ref[0 : e.shape[0], :] = e.astype(BF16)
    tail = jnp.concatenate([f[n * i : n * i + n] for i in range(4)], axis=1)
    o_ref[e.shape[0] :, :] = jnp.concatenate([tail, tail], axis=0).astype(BF16)


def finish(pos_ref, reach_ref, ek, e1, e3, e2, fk, f1, f3, f2, got, w_ref, t_ref, *, scale):
    e = ek[0].astype(F32)
    for ref in (e1, e3, e2):
        e = e + ref[0].astype(F32)
    m = e.shape[0]
    w_ref[...] = (e + got[0:m, :].astype(F32)) * scale
    f = fk[0]
    for ref in (f1, f3, f2):
        f = f + ref[0].astype(F32)
    n = f.shape[0] // 4
    tail = got[m:, :].astype(F32)[0:n]
    wide = f.shape[1]
    f = f + jnp.concatenate([tail[:, wide * i : wide * i + wide] for i in range(4)], axis=0)
    chan = pos_ref[0] * 2 + pos_ref[1]
    place = pos_ref[4]
    own_cols = iota((16, 8, 256), 1) == iota((16, 8, 256), 2) % 8
    row = iota((128, VN), 0)
    first = chan * 128 // GROUP
    limit = jnp.where(row < GROUP, reach_ref[first], reach_ref[first + 1])
    keep = place * VN + iota((128, VN), 1) < limit
    for d in range(2):
        v = iota((256, VN), 0) // 8
        e = (iota((256, VN), 1) == (v if d == 0 else (VN - 1) - v)).astype(F32)
        s = f[16 * d : 16 * d + 16, :]
        spread = jnp.broadcast_to(s[:, None, :], (16, 8, 256))
        spread = jnp.where(own_cols, spread, 0.0).reshape(128, 256)
        taps = lax.dot_general(
            spread, e, (((1,), (0,)), ((), ())),
            precision=lax.Precision.HIGHEST, preferred_element_type=F32,
        )
        t_ref[d] = jnp.where(keep, taps * scale, 0.0)


def swap(v, axis, mask):
    return lax.ppermute(v, axis, [(i, i ^ mask) for i in range(lax.axis_size(axis))])


def smem():
    return pl.BlockSpec(memory_space=pltpu.SMEM)


def call(body, out_shape, args, scalars=1, scratch=()):
    vmem = pl.BlockSpec(memory_space=pltpu.VMEM)
    return pl.pallas_call(
        body,
        out_shape=out_shape,
        in_specs=[smem()] * scalars + [vmem] * (len(args) - scalars),
        out_specs=jax.tree.map(lambda _: vmem, out_shape),
        scratch_shapes=list(scratch),
    )(*args)


def on_device_0(out_grad, out_weight, conv_input, gate_values, conv_output, filters, filter_reach):
    shape = jax.ShapeDtypeStruct
    rows, tok = conv_input.shape
    feats = out_grad.shape[1]
    seq_count = lax.axis_size("seq")
    place = lax.axis_index("seq").astype(jnp.int32)
    chan = lax.axis_index("chan").astype(jnp.int32)
    pos = jnp.stack([chan >> 1, chan & 1, place >> 3, (place >> 1) & 3, place])
    half = rows // 2
    scale = 1.0 / float(tok * seq_count) ** 0.5

    mine, other = call(gate_rows, [shape((half, tok), BF16)] * 2, (pos, conv_output, gate_values))
    own = jnp.concatenate([mine, swap(other, "seq", 1)], axis=1)
    og_core = swap(out_grad, "seq", 1)
    b1 = swap(own, "chan", 2)
    b3 = swap(own, "chan", 6)
    b2 = swap(own, "chan", 4)
    bx = swap(jnp.stack([own, b1, b2, b3]), "chan", 1)

    k, s1, s3, s2 = call(first_product, [shape((256, tok), BF16)] * 4, (pos, out_weight, out_grad))
    parts = [k, swap(s1, "chan", 2), swap(s3, "chan", 6), swap(s2, "chan", 4)]
    away = sum(p[128:].astype(F32) for p in parts).astype(BF16)
    got = swap(away, "chan", 1)
    grad_gated = sum(p[:128].astype(F32) for p in parts) + got.astype(F32)
    grad_gate = grad_gated * conv_output.astype(F32)
    grad_conv = (grad_gated * gate_values.astype(F32)).astype(BF16)

    halo_core = swap(grad_conv, "seq", 1)
    pairs = [(i, i + 1) for i in range(1, seq_count - 1, 2)]
    halo_out = lax.ppermute(grad_conv, "seq", pairs + [(b, a) for a, b in pairs])

    e = call(
        second_product,
        [shape((2, half, feats), BF16)] * 4,
        (pos, own, b1, b3, b2, bx, out_grad, og_core),
        scratch=[pltpu.VMEM((8, half, 2 * tok), BF16)],
    )
    e = [e[0], swap(e[1], "seq", 2), swap(e[2], "seq", 6), swap(e[3], "seq", 4)]

    grad_input, tap_sums = call(
        conv_grads,
        [shape((rows, tok), F32), shape((16, rows // 4, 256), F32)],
        (pos, filter_reach, grad_conv, halo_core, halo_out, filters, conv_input),
        scalars=2,
        scratch=[pltpu.VMEM((2, 256, 3 * tok), BF16), pltpu.VMEM((2, 2, 128, 2 * tok), BF16)],
    )
    f_got = swap(tap_sums[8:].astype(BF16), "seq", 1)
    piece = (2, rows // 4, 256)
    f = call(
        split_taps, [shape(piece, F32)] + [shape(piece, BF16)] * 3,
        (tap_sums, f_got), scalars=0,
    )
    f = [f[0], swap(f[1], "seq", 2), swap(f[2], "seq", 6), swap(f[3], "seq", 4)]
    last = call(last_send, shape((half + 16, feats), BF16), (*e, *f), scalars=0)
    got = swap(last, "seq", 8)
    grad_weight, grad_filters = call(
        functools.partial(finish, scale=scale),
        [shape((half, feats), F32), shape((2, rows, VN), F32)],
        (pos, filter_reach, *e, *f, got),
        scalars=2,
    )
    return (grad_input, grad_gate, grad_weight, grad_filters)


def solution(mesh):
    return jax.shard_map(
        on_device_0,
        mesh=mesh,
        in_specs=(
            P("seq", "chan"),
            P(None, "chan"),
            P("chan", "seq"),
            P("chan", "seq"),
            P("chan", "seq"),
            P(None, "chan", None),
            P(),
        ),
        out_specs=(P("chan", "seq"), P("chan", "seq"), P("seq", "chan"), P(None, "chan", "seq")),
        check_vma=False,
    )
```

```python
import functools

import jax
import jax.numpy as jnp
from jax import lax
from jax.experimental import pallas as pl
from jax.experimental.pallas import tpu as pltpu
from jax.sharding import PartitionSpec as P


GROUP = 64
VN = 32
F32 = jnp.float32
BF16 = jnp.bfloat16


def iota(shape, dim):
    return lax.broadcasted_iota(jnp.int32, shape, dim)


def dot(a, b, dims=(((1,), (0,)), ((), ()))):
    return lax.dot_general(a, b, dims, preferred_element_type=F32)


NT = (((1,), (1,)), ((), ()))


RELS = (0, 1, 3, 2)


def gate_rows(pos_ref, v_ref, g_ref, mine, other):
    half = mine.shape[0]
    core = pos_ref[4] % 2
    for ref, part in ((mine, core), (other, 1 - core)):
        band = pl.ds(pl.multiple_of(part * half, half), half)
        ref[...] = (v_ref[band, :].astype(F32) * g_ref[band, :].astype(F32)).astype(BF16)


def first_product(pos_ref, w_ref, og_ref, keep, send):
    z = pos_ref[0]
    x = pos_ref[1]
    og = og_ref[...]
    for i, rel in enumerate(RELS):
        w = [w_ref[pl.ds(((z ^ rel) * 2 + (x ^ a)) * 128, 128), :] for a in range(2)]
        p = dot(jnp.concatenate(w, axis=0), og, NT).astype(BF16)
        keep[128 * i : 128 * (i + 1), :] = p[:128]
        send[128 * i : 128 * (i + 1), :] = p[128:]


def middle_sums(k_ref, r_ref, *outs):
    n = k_ref.shape[0] // 4
    for i, ref in enumerate(outs):
        band = slice(n * i, n * i + n)
        ref[...] = (k_ref[band, :].astype(F32) + r_ref[band, :].astype(F32)).astype(ref.dtype)


def gate_grads(k_ref, r1, r3, r2, v_ref, g_ref, gate_ref, conv_ref):
    total = k_ref[...] + r1[...].astype(F32) + r3[...].astype(F32) + r2[...].astype(F32)
    gate_ref[...] = total * v_ref[...].astype(F32)
    conv_ref[...] = (total * g_ref[...].astype(F32)).astype(BF16)


def second_product(pos_ref, b0, b1, b3, b2, og_ref, ogs_ref, *refs):
    outs, g_ref = refs[:4], refs[4]
    for i, ref in enumerate((b0, b1, b2, b3)):
        g_ref[i] = ref[0]
        g_ref[4 + i] = ref[1]
    z = pos_ref[0]
    x = pos_ref[1]
    xh = pos_ref[2]
    y = pos_ref[3]
    tok = og_ref.shape[0]
    for ref, rel in zip(outs, RELS):
        for a in range(2):
            j = (xh ^ a) * 4 + (y ^ rel)
            g = g_ref[((j % 2) ^ x) * 4 + ((j // 2) ^ z)]
            ref[a] = (dot(g[:, :tok], og_ref[...]) + dot(g[:, tok:], ogs_ref[...])).astype(BF16)


def lagged(x, first, width):
    pair = [pltpu.roll(x, s % width, 1) if s % width else x for s in first]
    return jnp.concatenate(pair, axis=0).astype(BF16)


def conv_grads(pos_ref, reach_ref, gm_ref, gs_ref, gp_ref, f_ref, x_ref,
               o_ref, keep_ref, send_ref, h_ref, u_ref, t_ref):
    rows, n = gm_ref.shape
    width = 3 * n
    lanes = n // 128
    chan = pos_ref[0] * 2 + pos_ref[1]
    place = pos_ref[4]
    core0 = (place & 1) == 0
    own_rows = (iota((128, 256), 0) & 7) == (iota((128, 256), 1) & 7)
    ef = (iota((128, 256), 0) == (iota((128, 256), 1) >> 3)).astype(BF16)
    eb = (iota((128, 256), 0) == (VN - 1) - (iota((128, 256), 1) >> 3)).astype(BF16)
    own_cols = iota((16, 8, 256), 1) == (iota((16, 8, 256), 2) & 7)
    taps = f_ref.shape[2]
    lag = iota((8, taps), 1)

    def step(i, carry):
        base = pl.multiple_of(i * 16, 16)
        band = pl.ds(base, 16)
        gm = gm_ref[band, :].astype(F32)
        gs = gs_ref[band, :].astype(F32)
        gp = gp_ref[band, :].astype(F32)
        ext16 = jnp.concatenate([jnp.where(core0, gp, gs), gm, jnp.where(core0, gs, gp)], axis=1)
        own16 = x_ref[band, :].astype(F32)
        filt16 = [f_ref[d, band, :].astype(F32) for d in range(2)]
        inside = lag < reach_ref[(chan * rows + base) // GROUP]
        zero = jnp.zeros((8, n), F32)
        outs = []
        for h in range(2):
            ext = ext16[8 * h : 8 * h + 8]
            two = jnp.concatenate([ext, pltpu.roll(ext, width - 1, 1)], axis=0).astype(BF16)
            for k in range(VN // 2):
                moved = two if k == 0 else pltpu.roll(two, width - 2 * k, 1)
                h_ref[h, 16 * k : 16 * k + 16, :] = moved
            lhs = []
            for d, e in ((0, ef), (1, eb)):
                f8 = jnp.where(inside, filt16[d][8 * h : 8 * h + 8], 0.0)
                rolled = [f8 if b == 0 else pltpu.roll(f8, taps - 32 * b, 1) for b in range(4)]
                cut = [rolled[u % 4][:, 128 * (u // 4) : 128 * (u // 4) + 128] for u in range(16)]
                spread = dot(jnp.concatenate(cut, axis=0).astype(BF16), e)
                lhs.append(jnp.where(own_rows, spread, 0.0).astype(BF16))
            total = None
            for d in range(2):
                acc = [[None] * (lanes + (b > 0)) for b in range(4)]
                for j in range(lanes):
                    if d == 0:
                        lo, hi = (0, 64) if j == 0 else (64, 128) if j == lanes - 1 else (0, 128)
                    else:
                        lo, hi = (48, 128) if j == 0 else (0, 64) if j == lanes - 1 else (0, 128)
                    at = n * (1 - d) + 256 * j
                    p = dot(lhs[d][lo:hi], h_ref[h, :, at : at + 256])
                    for u in range(lo // 8, hi // 8):
                        a, b = divmod(u + d, 4)
                        for c in range(2):
                            q = 2 * j + c
                            slot = q - a if d == 0 else q - (lanes - (b > 0)) + a
                            if 0 <= slot < len(acc[b]):
                                part = p[8 * u - lo : 8 * u - lo + 8, 128 * c : 128 * c + 128]
                                acc[b][slot] = part if acc[b][slot] is None else acc[b][slot] + part
                for b in range(4):
                    line = jnp.concatenate(acc[b], axis=1)
                    if b and d == 0:
                        line = pltpu.roll(line, n + 128 - 32 * b, 1)[:, :n]
                    elif b:
                        line = pltpu.roll(line, 32 * b, 1)[:, 128:]
                    total = line if total is None else total + line
            outs.append(total)
            own = jnp.concatenate([zero, own16[8 * h : 8 * h + 8], zero], axis=1)
            bases = (
                (lagged(own, (0, 32), width), lagged(own, (64, 96), width)),
                (lagged(own, (-32, -64), width), lagged(own, (-96, -128), width)),
            )
            for d in range(2):
                for k in range(8):
                    start = n - 128 * (k // 2) if d == 0 else 128 * (k // 2)
                    u_ref[h, d, 16 * k : 16 * k + 16, :] = bases[d][k % 2][:, start : start + 2 * n]
            for d in range(2):
                start = n * (1 - d)
                cross = dot(u_ref[h, d], h_ref[h, :, start : start + 2 * n], NT)
                sums = jnp.sum(jnp.where(own_cols, cross.reshape(16, 8, 256), 0.0), axis=1)
                row = d * (rows // 8) + 2 * i + h
                for u in range(16):
                    r = u ^ place
                    slot = (r & 1) * 8 + ((r >> 1) & 3) * 2 + (r >> 3)
                    t_ref[slot, pl.ds(row, 1), :] = sums[u : u + 1]
        o_ref[band, :] = jnp.concatenate(outs, axis=0)
        return carry

    lax.fori_loop(0, rows // 16, step, 0)
    keep_ref[...] = t_ref[0:8]
    send_ref[...] = t_ref[8:16].astype(BF16)


def split_taps(t_ref, got_ref, k, s1, s3, s2):
    for rel, ref in ((0, k), (1, s1), (3, s3), (2, s2)):
        both = t_ref[2 * rel : 2 * rel + 2] + got_ref[2 * rel : 2 * rel + 2].astype(F32)
        ref[...] = both.astype(ref.dtype)


def last_send(ek, e1, e3, e2, fk, f1, f3, f2, o_ref):
    e = ek[1].astype(F32)
    for ref in (e1, e3, e2):
        e = e + ref[1].astype(F32)
    f = fk[1]
    for ref in (f1, f3, f2):
        f = f + ref[1].astype(F32)
    n = f.shape[0] // 4
    o_ref[0 : e.shape[0], :] = e.astype(BF16)
    tail = jnp.concatenate([f[n * i : n * i + n] for i in range(4)], axis=1)
    o_ref[e.shape[0] :, :] = jnp.concatenate([tail, tail], axis=0).astype(BF16)


def finish(pos_ref, reach_ref, ek, e1, e3, e2, fk, f1, f3, f2, got, w_ref, t_ref, *, scale):
    e = ek[0].astype(F32)
    for ref in (e1, e3, e2):
        e = e + ref[0].astype(F32)
    m = e.shape[0]
    w_ref[...] = (e + got[0:m, :].astype(F32)) * scale
    f = fk[0]
    for ref in (f1, f3, f2):
        f = f + ref[0].astype(F32)
    n = f.shape[0] // 4
    tail = got[m:, :].astype(F32)[0:n]
    wide = f.shape[1]
    f = f + jnp.concatenate([tail[:, wide * i : wide * i + wide] for i in range(4)], axis=0)
    chan = pos_ref[0] * 2 + pos_ref[1]
    place = pos_ref[4]
    own_cols = iota((16, 8, 256), 1) == (iota((16, 8, 256), 2) & 7)
    first = chan * 128 // GROUP
    limit = jnp.where(iota((VN, 128), 1) < GROUP, reach_ref[first], reach_ref[first + 1])
    keep = place * VN + iota((VN, 128), 0) < limit
    for d in range(2):
        v = iota((VN, 256), 1) >> 3
        e = (iota((VN, 256), 0) == (v if d == 0 else (VN - 1) - v)).astype(BF16)
        part = f[16 * d : 16 * d + 16, :]
        spread = jnp.broadcast_to(part[:, None, :], (16, 8, 256))
        spread = jnp.where(own_cols, spread, 0.0).reshape(128, 256)
        high = spread.astype(BF16)
        low = (spread - high.astype(F32)).astype(BF16)
        t_ref[d] = jnp.where(keep, (dot(e, high, NT) + dot(e, low, NT)) * scale, 0.0)


def swap(v, axis, mask):
    return lax.ppermute(v, axis, [(i, i ^ mask) for i in range(lax.axis_size(axis))])


def smem():
    return pl.BlockSpec(memory_space=pltpu.SMEM)


def call(body, out_shape, args, scalars=1, scratch=(), limit=16):
    vmem = pl.BlockSpec(memory_space=pltpu.VMEM)
    held = [pltpu.with_memory_space_constraint(a, pltpu.VMEM) for a in args[scalars:]]
    return pl.pallas_call(
        body,
        out_shape=out_shape,
        in_specs=[smem()] * scalars + [vmem] * len(held),
        out_specs=jax.tree.map(lambda _: vmem, out_shape),
        scratch_shapes=list(scratch),
        compiler_params=pltpu.CompilerParams(vmem_limit_bytes=limit << 20),
    )(*args[:scalars], *held)


def on_device_0(out_grad, out_weight, conv_input, gate_values, conv_output, filters, filter_reach):
    shape = jax.ShapeDtypeStruct
    rows, tok = conv_input.shape
    feats = out_grad.shape[1]
    seq_count = lax.axis_size("seq")
    place = lax.axis_index("seq").astype(jnp.int32)
    chan = lax.axis_index("chan").astype(jnp.int32)
    pos = jnp.stack([chan >> 1, chan & 1, place >> 3, (place >> 1) & 3, place])
    half = rows // 2
    scale = 1.0 / float(tok * seq_count) ** 0.5

    mine, other = call(gate_rows, [shape((half, tok), BF16)] * 2, (pos, conv_output, gate_values))
    own = jnp.concatenate([mine, swap(other, "seq", 1)], axis=1)
    og_core = swap(out_grad, "seq", 1)
    pair = jnp.stack([own, swap(own, "chan", 1)])
    b1 = swap(pair, "chan", 2)
    b3 = swap(pair, "chan", 6)
    b2 = swap(pair, "chan", 4)

    keep, send = call(
        first_product, [shape((rows * 4, tok), BF16)] * 2, (pos, out_weight, out_grad)
    )
    keep, s1, s3, s2 = call(
        middle_sums,
        [shape((rows, tok), F32)] + [shape((rows, tok), BF16)] * 3,
        (keep, swap(send, "chan", 1)),
        scalars=0,
    )
    s1, s3, s2 = swap(s1, "chan", 2), swap(s3, "chan", 6), swap(s2, "chan", 4)
    grad_gate, grad_conv = call(
        gate_grads,
        [shape((rows, tok), F32), shape((rows, tok), BF16)],
        (keep, s1, s3, s2, conv_output, gate_values),
        scalars=0,
    )

    halo_core = swap(grad_conv, "seq", 1)
    pairs = [(i, i + 1) for i in range(1, seq_count - 1, 2)]
    halo_out = lax.ppermute(grad_conv, "seq", pairs + [(b, a) for a, b in pairs])

    e = call(
        second_product,
        [shape((2, half, feats), BF16)] * 4,
        (pos, pair, b1, b3, b2, out_grad, og_core),
        scratch=[pltpu.VMEM((8, half, 2 * tok), BF16)],
    )
    e = [e[0], swap(e[1], "seq", 2), swap(e[2], "seq", 6), swap(e[3], "seq", 4)]

    grad_input, tap_keep, tap_send = call(
        conv_grads,
        [
            shape((rows, tok), F32),
            shape((8, rows // 4, 256), F32),
            shape((8, rows // 4, 256), BF16),
        ],
        (pos, filter_reach, grad_conv, halo_core, halo_out, filters, conv_input),
        scalars=2,
        scratch=[
            pltpu.VMEM((2, 256, 3 * tok), BF16),
            pltpu.VMEM((2, 2, 128, 2 * tok), BF16),
            pltpu.VMEM((16, rows // 4, 256), F32),
        ],
    )
    f_got = swap(tap_send, "seq", 1)
    piece = (2, rows // 4, 256)
    f = call(
        split_taps, [shape(piece, F32)] + [shape(piece, BF16)] * 3,
        (tap_keep, f_got), scalars=0,
    )
    f = [f[0], swap(f[1], "seq", 2), swap(f[2], "seq", 6), swap(f[3], "seq", 4)]
    last = call(last_send, shape((half + 16, feats), BF16), (*e, *f), scalars=0)
    got = swap(last, "seq", 8)
    grad_weight, grad_filters = call(
        functools.partial(finish, scale=scale),
        [shape((half, feats), F32), shape((2, VN, rows), F32)],
        (pos, filter_reach, *e, *f, got),
        scalars=2,
    )
    return (grad_input, grad_gate, grad_weight, jnp.transpose(grad_filters, (0, 2, 1)))


def solution(mesh):
    return jax.shard_map(
        on_device_0,
        mesh=mesh,
        in_specs=(
            P("seq", "chan"),
            P(None, "chan"),
            P("chan", "seq"),
            P("chan", "seq"),
            P("chan", "seq"),
            P(None, "chan", None),
            P(),
        ),
        out_specs=(P("chan", "seq"), P("chan", "seq"), P("seq", "chan"), P(None, "chan", "seq")),
        check_vma=False,
    )
```

```python
import functools

import jax
import jax.numpy as jnp
from jax import lax
from jax.experimental import pallas as pl
from jax.experimental.pallas import tpu as pltpu
from jax.sharding import PartitionSpec as P


GROUP = 64
VN = 32
F32 = jnp.float32
BF16 = jnp.bfloat16


def iota(shape, dim):
    return lax.broadcasted_iota(jnp.int32, shape, dim)


def dot(a, b, dims=(((1,), (0,)), ((), ()))):
    return lax.dot_general(a, b, dims, preferred_element_type=F32)


NT = (((1,), (1,)), ((), ()))


RELS = (0, 1, 3, 2)


def gate_rows(pos_ref, v_hbm, g_hbm, mine, other, v_ref, g_ref, sems):
    loads = [
        pltpu.make_async_copy(v_hbm, v_ref, sems.at[0]),
        pltpu.make_async_copy(g_hbm, g_ref, sems.at[1]),
    ]
    for load in loads:
        load.start()
    for load in loads:
        load.wait()
    half = mine.shape[0]
    core = pos_ref[4] & 1
    for ref, part in ((mine, core), (other, 1 - core)):
        band = pl.ds(pl.multiple_of(part * half, half), half)
        ref[...] = (v_ref[band, :].astype(F32) * g_ref[band, :].astype(F32)).astype(BF16)


def first_product(pos_ref, w_hbm, og_hbm, keep, send, w_ref, og_ref, sems):
    z = pos_ref[0]
    x = pos_ref[1]
    og_load = pltpu.make_async_copy(og_hbm, og_ref, sems.at[8])
    og_load.start()
    loads = []
    for i, rel in enumerate(RELS):
        for a in range(2):
            rows = pl.ds(pl.multiple_of(((z ^ rel) * 2 + (x ^ a)) * 128, 128), 128)
            part = w_ref.at[i, 128 * a : 128 * (a + 1)]
            loads.append(pltpu.make_async_copy(w_hbm.at[rows], part, sems.at[2 * i + a]))
            loads[-1].start()
    og_load.wait()
    og = og_ref[...]
    for i in range(4):
        loads[2 * i].wait()
        loads[2 * i + 1].wait()
        p = dot(w_ref[i], og, NT).astype(BF16)
        keep[128 * i : 128 * (i + 1), :] = p[:128]
        send[128 * i : 128 * (i + 1), :] = p[128:]


def middle_sums(k_ref, r_ref, *outs):
    n = k_ref.shape[0] // 4
    for i, ref in enumerate(outs):
        band = slice(n * i, n * i + n)
        ref[...] = (k_ref[band, :].astype(F32) + r_ref[band, :].astype(F32)).astype(ref.dtype)


def gate_grads(k_ref, r1, r3, r2, v_ref, g_ref, gate_ref, conv_ref):
    total = k_ref[...] + r1[...].astype(F32) + r3[...].astype(F32) + r2[...].astype(F32)
    gate_ref[...] = total * v_ref[...].astype(F32)
    conv_ref[...] = (total * g_ref[...].astype(F32)).astype(BF16)


def second_product(pos_ref, b0, b1, b3, b2, og_ref, ogs_ref, *refs):
    outs, g_ref = refs[:4], refs[4]
    for i, ref in enumerate((b0, b1, b2, b3)):
        g_ref[i] = ref[0]
        g_ref[4 + i] = ref[1]
    z = pos_ref[0]
    x = pos_ref[1]
    xh = pos_ref[2]
    y = pos_ref[3]
    tok = og_ref.shape[0]
    for ref, rel in zip(outs, RELS):
        for a in range(2):
            j = (xh ^ a) * 4 + (y ^ rel)
            g = g_ref[((j % 2) ^ x) * 4 + ((j // 2) ^ z)]
            ref[a] = (dot(g[:, :tok], og_ref[...]) + dot(g[:, tok:], ogs_ref[...])).astype(BF16)


def lagged(x, shifts, width):
    pair = [pltpu.roll(x, s % width, 1) if s % width else x for s in shifts]
    return jnp.concatenate(pair, axis=0).astype(BF16)


def prepare(pos_ref, reach_ref, f_ref, x_ref, l_ref, ui_ref, uo_ref):
    rows, n = x_ref.shape
    width = 3 * n
    chan = pos_ref[0] * 2 + pos_ref[1]
    own_rows = (iota((128, 256), 0) & 7) == (iota((128, 256), 1) & 7)
    ef = (iota((128, 256), 0) == (iota((128, 256), 1) >> 3)).astype(BF16)
    eb = (iota((128, 256), 0) == (VN - 1) - (iota((128, 256), 1) >> 3)).astype(BF16)
    taps = f_ref.shape[2]
    lag = iota((8, taps), 1)

    def step(i, carry):
        base = pl.multiple_of(i * 16, 16)
        band = pl.ds(base, 16)
        own16 = x_ref[band, :].astype(F32)
        filt16 = [f_ref[d, band, :].astype(F32) for d in range(2)]
        inside = lag < reach_ref[(chan * rows + base) // GROUP]
        zero = jnp.zeros((8, n), F32)
        for h in range(2):
            group = 2 * i + h
            for d, e in ((0, ef), (1, eb)):
                f8 = jnp.where(inside, filt16[d][8 * h : 8 * h + 8], 0.0)
                rolled = [f8 if b == 0 else pltpu.roll(f8, taps - 32 * b, 1) for b in range(4)]
                cut = [rolled[u % 4][:, 128 * (u // 4) : 128 * (u // 4) + 128] for u in range(16)]
                spread = dot(jnp.concatenate(cut, axis=0).astype(BF16), e)
                l_ref[group, d] = jnp.where(own_rows, spread, 0.0).astype(BF16)
            own = jnp.concatenate([zero, own16[8 * h : 8 * h + 8], zero], axis=1)
            bases = (
                (lagged(own, (0, 32), width), lagged(own, (64, 96), width)),
                (lagged(own, (-32, -64), width), lagged(own, (-96, -128), width)),
            )
            for d in range(2):
                for k in range(8):
                    start = n - 128 * (k // 2) if d == 0 else 128 * (k // 2)
                    part = bases[d][k % 2][:, start : start + 2 * n]
                    inner, outer = (part[:, :n], part[:, n:]) if d == 0 else (part[:, n:], part[:, :n])
                    at = 128 * d + 16 * k
                    ui_ref[group, at : at + 16, :] = inner
                    uo_ref[group, at : at + 16, :] = outer
        return carry

    lax.fori_loop(0, rows // 16, step, 0)


def conv_grads(pos_ref, gm_ref, gs_ref, gp_ref, l_ref, ui_ref, uo_ref,
               o_ref, keep_ref, send_ref, h_ref, t_ref):
    rows, n = gm_ref.shape
    width = 3 * n
    lanes = n // 128
    place = pos_ref[4]
    core0 = (place & 1) == 0
    own_cols = iota((16, 8, 256), 1) == (iota((16, 8, 256), 2) & 7)

    def step(i, carry):
        band = pl.ds(pl.multiple_of(i * 16, 16), 16)
        gm = gm_ref[band, :].astype(F32)
        gs = gs_ref[band, :].astype(F32)
        gp = gp_ref[band, :].astype(F32)
        ext16 = jnp.concatenate([jnp.where(core0, gp, gs), gm, jnp.where(core0, gs, gp)], axis=1)
        outs = []
        for h in range(2):
            group = 2 * i + h
            ext = ext16[8 * h : 8 * h + 8]
            two = jnp.concatenate([ext, pltpu.roll(ext, width - 1, 1)], axis=0).astype(BF16)
            for k in range(VN // 2):
                moved = two if k == 0 else pltpu.roll(two, width - 2 * k, 1)
                h_ref[h, 16 * k : 16 * k + 16, :] = moved
            total = None
            for d in range(2):
                acc = [[None] * (lanes + (b > 0)) for b in range(4)]
                for j in range(lanes):
                    if d == 0:
                        lo, hi = (0, 64) if j == 0 else (64, 128) if j == lanes - 1 else (0, 128)
                    else:
                        lo, hi = (48, 128) if j == 0 else (0, 64) if j == lanes - 1 else (0, 128)
                    at = n * (1 - d) + 256 * j
                    p = dot(l_ref[group, d, lo:hi, :], h_ref[h, :, at : at + 256])
                    for u in range(lo // 8, hi // 8):
                        a, b = divmod(u + d, 4)
                        for c in range(2):
                            q = 2 * j + c
                            slot = q - a if d == 0 else q - (lanes - (b > 0)) + a
                            if 0 <= slot < len(acc[b]):
                                part = p[8 * u - lo : 8 * u - lo + 8, 128 * c : 128 * c + 128]
                                acc[b][slot] = part if acc[b][slot] is None else acc[b][slot] + part
                for b in range(4):
                    line = jnp.concatenate(acc[b], axis=1)
                    if b and d == 0:
                        line = pltpu.roll(line, n + 128 - 32 * b, 1)[:, :n]
                    elif b:
                        line = pltpu.roll(line, 32 * b, 1)[:, 128:]
                    total = line if total is None else total + line
            outs.append(total)
            inner = dot(ui_ref[group], h_ref[h, :, n : 2 * n], NT)
            for d in range(2):
                start = 2 * n * (1 - d)
                cross = inner[128 * d : 128 * d + 128] + dot(
                    uo_ref[group, 128 * d : 128 * d + 128, :], h_ref[h, :, start : start + n], NT
                )
                sums = jnp.sum(jnp.where(own_cols, cross.reshape(16, 8, 256), 0.0), axis=1)
                row = d * (rows // 8) + group
                for u in range(16):
                    r = u ^ place
                    slot = (r & 1) * 8 + ((r >> 1) & 3) * 2 + (r >> 3)
                    t_ref[slot, pl.ds(row, 1), :] = sums[u : u + 1]
        o_ref[band, :] = jnp.concatenate(outs, axis=0)
        return carry

    lax.fori_loop(0, rows // 16, step, 0)
    keep_ref[...] = t_ref[0:8]
    send_ref[...] = t_ref[8:16].astype(BF16)


def split_taps(t_ref, got_ref, k, s1, s3, s2):
    for rel, ref in ((0, k), (1, s1), (3, s3), (2, s2)):
        both = t_ref[2 * rel : 2 * rel + 2] + got_ref[2 * rel : 2 * rel + 2].astype(F32)
        ref[...] = both.astype(ref.dtype)


def sum_pieces(k, r1, r3, r2, keep, send):
    for ref, i in ((keep, 0), (send, 1)):
        total = k[i].astype(F32)
        for r in (r1, r3, r2):
            total = total + r[i].astype(F32)
        ref[...] = total.astype(ref.dtype)


def finish_rows(keep, got, o_ref, *, scale):
    o_ref[...] = (keep[...] + got[...].astype(F32)) * scale


def finish_taps(pos_ref, reach_ref, part_ref, got, t_ref, *, scale):
    f = part_ref[...] + got[...].astype(F32)
    chan = pos_ref[0] * 2 + pos_ref[1]
    place = pos_ref[4]
    own_cols = iota((16, 8, 256), 1) == (iota((16, 8, 256), 2) & 7)
    first = chan * 128 // GROUP
    limit = jnp.where(iota((VN, 128), 1) < GROUP, reach_ref[first], reach_ref[first + 1])
    inside = place * VN + iota((VN, 128), 0) < limit
    for d in range(2):
        v = iota((VN, 256), 1) >> 3
        e = (iota((VN, 256), 0) == (v if d == 0 else (VN - 1) - v)).astype(BF16)
        part = f[16 * d : 16 * d + 16, :]
        spread = jnp.broadcast_to(part[:, None, :], (16, 8, 256))
        spread = jnp.where(own_cols, spread, 0.0).reshape(128, 256)
        high = spread.astype(BF16)
        low = (spread - high.astype(F32)).astype(BF16)
        t_ref[d] = jnp.where(inside, (dot(e, high, NT) + dot(e, low, NT)) * scale, 0.0)


def swap(v, axis, mask):
    return lax.ppermute(v, axis, [(i, i ^ mask) for i in range(lax.axis_size(axis))])


def smem():
    return pl.BlockSpec(memory_space=pltpu.SMEM)


def call(body, out_shape, args, scalars=1, scratch=(), limit=16, held_in=pltpu.VMEM):
    vmem = pl.BlockSpec(memory_space=pltpu.VMEM)
    where = pl.BlockSpec(memory_space=held_in)
    held = [pltpu.with_memory_space_constraint(a, held_in) for a in args[scalars:]]
    return pl.pallas_call(
        body,
        out_shape=out_shape,
        in_specs=[smem()] * scalars + [where] * len(held),
        out_specs=jax.tree.map(lambda _: vmem, out_shape),
        scratch_shapes=list(scratch),
        compiler_params=pltpu.CompilerParams(vmem_limit_bytes=limit << 20),
    )(*args[:scalars], *held)


def on_device_0(out_grad, out_weight, conv_input, gate_values, conv_output, filters, filter_reach):
    shape = jax.ShapeDtypeStruct
    rows, tok = conv_input.shape
    feats = out_grad.shape[1]
    seq_count = lax.axis_size("seq")
    place = lax.axis_index("seq").astype(jnp.int32)
    chan = lax.axis_index("chan").astype(jnp.int32)
    pos = jnp.stack([chan >> 1, chan & 1, place >> 3, (place >> 1) & 3, place])
    half = rows // 2
    scale = 1.0 / float(tok * seq_count) ** 0.5

    mine, other = call(
        gate_rows,
        [shape((half, tok), BF16)] * 2,
        (pos, conv_output, gate_values),
        scratch=[pltpu.VMEM((rows, tok), BF16)] * 2 + [pltpu.SemaphoreType.DMA((2,))],
        held_in=pltpu.HBM,
    )
    own = jnp.concatenate([mine, swap(other, "seq", 1)], axis=1)
    og_core = swap(out_grad, "seq", 1)
    pair = jnp.stack([own, swap(own, "chan", 1)])
    b1 = swap(pair, "chan", 2)
    b3 = swap(pair, "chan", 6)
    b2 = swap(pair, "chan", 4)

    keep, send = call(
        first_product,
        [shape((rows * 4, tok), BF16)] * 2,
        (pos, out_weight, out_grad),
        scratch=[
            pltpu.VMEM((4, 2 * rows, feats), BF16),
            pltpu.VMEM((tok, feats), BF16),
            pltpu.SemaphoreType.DMA((9,)),
        ],
        held_in=pltpu.HBM,
    )
    keep, s1, s3, s2 = call(
        middle_sums,
        [shape((rows, tok), F32)] + [shape((rows, tok), BF16)] * 3,
        (keep, swap(send, "chan", 1)),
        scalars=0,
    )
    s1, s3, s2 = swap(s1, "chan", 2), swap(s3, "chan", 6), swap(s2, "chan", 4)
    grad_gate, grad_conv = call(
        gate_grads,
        [shape((rows, tok), F32), shape((rows, tok), BF16)],
        (keep, s1, s3, s2, conv_output, gate_values),
        scalars=0,
    )

    halo_core = swap(grad_conv, "seq", 1)
    pairs = [(i, i + 1) for i in range(1, seq_count - 1, 2)]
    halo_out = lax.ppermute(grad_conv, "seq", pairs + [(b, a) for a, b in pairs])

    e = call(
        second_product,
        [shape((2, half, feats), BF16)] * 4,
        (pos, pair, b1, b3, b2, out_grad, og_core),
        scratch=[pltpu.VMEM((8, half, 2 * tok), BF16)],
    )
    e = [e[0], swap(e[1], "seq", 2), swap(e[2], "seq", 6), swap(e[3], "seq", 4)]

    groups = rows // 8
    prepared = call(
        prepare,
        [
            shape((groups, 2, 128, 256), BF16),
            shape((groups, 256, tok), BF16),
            shape((groups, 256, tok), BF16),
        ],
        (pos, filter_reach, filters, conv_input),
        scalars=2,
    )
    grad_input, tap_keep, tap_send = call(
        conv_grads,
        [
            shape((rows, tok), F32),
            shape((8, rows // 4, 256), F32),
            shape((8, rows // 4, 256), BF16),
        ],
        (pos, grad_conv, halo_core, halo_out, *prepared),
        scratch=[
            pltpu.VMEM((2, 256, 3 * tok), BF16),
            pltpu.VMEM((16, rows // 4, 256), F32),
        ],
    )
    f_got = swap(tap_send, "seq", 1)
    piece = (2, rows // 4, 256)
    f = call(
        split_taps, [shape(piece, F32)] + [shape(piece, BF16)] * 3,
        (tap_keep, f_got), scalars=0,
    )
    f = [f[0], swap(f[1], "seq", 2), swap(f[2], "seq", 6), swap(f[3], "seq", 4)]
    e_keep, e_send = call(
        sum_pieces, [shape((half, feats), F32), shape((half, feats), BF16)], e, scalars=0
    )
    e_got = swap(e_send, "seq", 8)
    f_keep, f_send = call(sum_pieces, [shape(piece[1:], F32), shape(piece[1:], BF16)], f, scalars=0)
    f_got = swap(f_send, "seq", 8)
    grad_weight = call(
        functools.partial(finish_rows, scale=scale),
        shape((half, feats), F32),
        (e_keep, e_got),
        scalars=0,
    )
    grad_filters = call(
        functools.partial(finish_taps, scale=scale),
        shape((2, VN, rows), F32),
        (pos, filter_reach, f_keep, f_got),
        scalars=2,
    )
    return (grad_input, grad_gate, grad_weight, jnp.transpose(grad_filters, (0, 2, 1)))


def solution(mesh):
    return jax.shard_map(
        on_device_0,
        mesh=mesh,
        in_specs=(
            P("seq", "chan"),
            P(None, "chan"),
            P("chan", "seq"),
            P("chan", "seq"),
            P("chan", "seq"),
            P(None, "chan", None),
            P(),
        ),
        out_specs=(P("chan", "seq"), P("chan", "seq"), P("seq", "chan"), P(None, "chan", "seq")),
        check_vma=False,
    )
```

```python
import functools

import jax
import jax.numpy as jnp
from jax import lax
from jax.experimental import pallas as pl
from jax.experimental.pallas import tpu as pltpu
from jax.sharding import PartitionSpec as P


GROUP = 64
VN = 32
F32 = jnp.float32
BF16 = jnp.bfloat16


def iota(shape, dim):
    return lax.broadcasted_iota(jnp.int32, shape, dim)


def dot(a, b, dims=(((1,), (0,)), ((), ()))):
    return lax.dot_general(a, b, dims, preferred_element_type=F32)


NT = (((1,), (1,)), ((), ()))


RELS = (0, 1, 3, 2)


def gate_rows(pos_ref, v_hbm, g_hbm, mine, other, v_ref, g_ref, sems):
    loads = [
        pltpu.make_async_copy(v_hbm, v_ref, sems.at[0]),
        pltpu.make_async_copy(g_hbm, g_ref, sems.at[1]),
    ]
    for load in loads:
        load.start()
    for load in loads:
        load.wait()
    half = mine.shape[0]
    core = pos_ref[4] & 1
    for ref, part in ((mine, core), (other, 1 - core)):
        band = pl.ds(pl.multiple_of(part * half, half), half)
        ref[...] = (v_ref[band, :].astype(F32) * g_ref[band, :].astype(F32)).astype(BF16)


def first_product(pos_ref, w_hbm, og_hbm, keep, send, w_ref, og_ref, sems):
    z = pos_ref[0]
    x = pos_ref[1]
    og_load = pltpu.make_async_copy(og_hbm, og_ref, sems.at[8])
    og_load.start()
    loads = []
    for i, rel in enumerate(RELS):
        for a in range(2):
            rows = pl.ds(pl.multiple_of(((z ^ rel) * 2 + (x ^ a)) * 128, 128), 128)
            part = w_ref.at[i, 128 * a : 128 * (a + 1)]
            loads.append(pltpu.make_async_copy(w_hbm.at[rows], part, sems.at[2 * i + a]))
            loads[-1].start()
    og_load.wait()
    og = og_ref[...]
    for i in range(4):
        loads[2 * i].wait()
        loads[2 * i + 1].wait()
        p = dot(w_ref[i], og, NT).astype(BF16)
        keep[128 * i : 128 * (i + 1), :] = p[:128]
        send[128 * i : 128 * (i + 1), :] = p[128:]


def middle_sums(k_ref, r_ref, *outs):
    n = k_ref.shape[0] // 4
    for i, ref in enumerate(outs):
        band = slice(n * i, n * i + n)
        ref[...] = (k_ref[band, :].astype(F32) + r_ref[band, :].astype(F32)).astype(ref.dtype)


def gate_grads(k_ref, r1, r3, r2, v_ref, g_ref, gate_ref, conv_ref):
    total = k_ref[...] + r1[...].astype(F32) + r3[...].astype(F32) + r2[...].astype(F32)
    gate_ref[...] = total * v_ref[...].astype(F32)
    conv_ref[...] = (total * g_ref[...].astype(F32)).astype(BF16)


def second_product(pos_ref, own, rx, own1, rx3, owns, rxs, og_ref, ogs_ref, *refs):
    outs, g_ref = refs[:4], refs[4]
    pieces = (own, own1, owns.at[1], owns.at[0], rx, rxs.at[0], rxs.at[1], rx3)
    for i, ref in enumerate(pieces):
        g_ref[i] = ref[...]
    z = pos_ref[0]
    x = pos_ref[1]
    xh = pos_ref[2]
    y = pos_ref[3]
    tok = og_ref.shape[0]
    for ref, rel in zip(outs, RELS):
        for a in range(2):
            j = (xh ^ a) * 4 + (y ^ rel)
            g = g_ref[((j % 2) ^ x) * 4 + ((j // 2) ^ z)]
            ref[a] = (dot(g[:, :tok], og_ref[...]) + dot(g[:, tok:], ogs_ref[...])).astype(BF16)


def lagged(x, shifts, width):
    pair = [pltpu.roll(x, s % width, 1) if s % width else x for s in shifts]
    return jnp.concatenate(pair, axis=0).astype(BF16)


def prepare(pos_ref, reach_ref, f_ref, x_ref, l_ref, ui_ref, uo_ref):
    rows, n = x_ref.shape
    width = 3 * n
    chan = pos_ref[0] * 2 + pos_ref[1]
    own_rows = (iota((128, 256), 0) & 7) == (iota((128, 256), 1) & 7)
    ef = (iota((128, 256), 0) == (iota((128, 256), 1) >> 3)).astype(BF16)
    eb = (iota((128, 256), 0) == (VN - 1) - (iota((128, 256), 1) >> 3)).astype(BF16)
    taps = f_ref.shape[2]
    lag = iota((8, taps), 1)

    def step(i, carry):
        base = pl.multiple_of(i * 16, 16)
        band = pl.ds(base, 16)
        own16 = x_ref[band, :].astype(F32)
        filt16 = [f_ref[d, band, :].astype(F32) for d in range(2)]
        inside = lag < reach_ref[(chan * rows + base) // GROUP]
        zero = jnp.zeros((8, n), F32)
        for h in range(2):
            group = 2 * i + h
            for d, e in ((0, ef), (1, eb)):
                f8 = jnp.where(inside, filt16[d][8 * h : 8 * h + 8], 0.0)
                rolled = [f8 if b == 0 else pltpu.roll(f8, taps - 32 * b, 1) for b in range(4)]
                cut = [rolled[u % 4][:, 128 * (u // 4) : 128 * (u // 4) + 128] for u in range(16)]
                spread = dot(jnp.concatenate(cut, axis=0).astype(BF16), e)
                l_ref[group, d] = jnp.where(own_rows, spread, 0.0).astype(BF16)
            own = jnp.concatenate([zero, own16[8 * h : 8 * h + 8], zero], axis=1)
            bases = (
                (lagged(own, (0, 32), width), lagged(own, (64, 96), width)),
                (lagged(own, (-32, -64), width), lagged(own, (-96, -128), width)),
            )
            for d in range(2):
                for k in range(8):
                    start = n - 128 * (k // 2) if d == 0 else 128 * (k // 2)
                    part = bases[d][k % 2][:, start : start + 2 * n]
                    inner, outer = (part[:, :n], part[:, n:]) if d == 0 else (part[:, n:], part[:, :n])
                    at = 128 * d + 16 * k
                    ui_ref[group, at : at + 16, :] = inner
                    uo_ref[group, at : at + 16, :] = outer
        return carry

    lax.fori_loop(0, rows // 16, step, 0)


def conv_grads(pos_ref, gm_ref, gs_ref, gp_ref, l_ref, ui_ref, uo_ref,
               o_ref, keep_ref, send_ref, h_ref, t_ref):
    rows, n = gm_ref.shape
    width = 3 * n
    lanes = n // 128
    place = pos_ref[4]
    core0 = (place & 1) == 0
    own_cols = iota((16, 8, 256), 1) == (iota((16, 8, 256), 2) & 7)

    def step(i, carry):
        band = pl.ds(pl.multiple_of(i * 16, 16), 16)
        gm = gm_ref[band, :].astype(F32)
        gs = gs_ref[band, :].astype(F32)
        gp = gp_ref[band, :].astype(F32)
        ext16 = jnp.concatenate([jnp.where(core0, gp, gs), gm, jnp.where(core0, gs, gp)], axis=1)
        outs = []
        for h in range(2):
            group = 2 * i + h
            ext = ext16[8 * h : 8 * h + 8]
            two = jnp.concatenate([ext, pltpu.roll(ext, width - 1, 1)], axis=0).astype(BF16)
            for k in range(VN // 2):
                moved = two if k == 0 else pltpu.roll(two, width - 2 * k, 1)
                h_ref[h, 16 * k : 16 * k + 16, :] = moved
            total = None
            for d in range(2):
                acc = [[None] * (lanes + (b > 0)) for b in range(4)]
                for j in range(lanes):
                    if d == 0:
                        lo, hi = (0, 64) if j == 0 else (64, 128) if j == lanes - 1 else (0, 128)
                    else:
                        lo, hi = (48, 128) if j == 0 else (0, 64) if j == lanes - 1 else (0, 128)
                    at = n * (1 - d) + 256 * j
                    p = dot(l_ref[group, d, lo:hi, :], h_ref[h, :, at : at + 256])
                    for u in range(lo // 8, hi // 8):
                        a, b = divmod(u + d, 4)
                        for c in range(2):
                            q = 2 * j + c
                            slot = q - a if d == 0 else q - (lanes - (b > 0)) + a
                            if 0 <= slot < len(acc[b]):
                                part = p[8 * u - lo : 8 * u - lo + 8, 128 * c : 128 * c + 128]
                                acc[b][slot] = part if acc[b][slot] is None else acc[b][slot] + part
                for b in range(4):
                    line = jnp.concatenate(acc[b], axis=1)
                    if b and d == 0:
                        line = pltpu.roll(line, n + 128 - 32 * b, 1)[:, :n]
                    elif b:
                        line = pltpu.roll(line, 32 * b, 1)[:, 128:]
                    total = line if total is None else total + line
            outs.append(total)
            inner = dot(ui_ref[group], h_ref[h, :, n : 2 * n], NT)
            for d in range(2):
                start = 2 * n * (1 - d)
                cross = inner[128 * d : 128 * d + 128] + dot(
                    uo_ref[group, 128 * d : 128 * d + 128, :], h_ref[h, :, start : start + n], NT
                )
                sums = jnp.sum(jnp.where(own_cols, cross.reshape(16, 8, 256), 0.0), axis=1)
                row = d * (rows // 8) + group
                for u in range(16):
                    r = u ^ place
                    slot = (r & 1) * 8 + ((r >> 1) & 3) * 2 + (r >> 3)
                    t_ref[slot, pl.ds(row, 1), :] = sums[u : u + 1]
        o_ref[band, :] = jnp.concatenate(outs, axis=0)
        return carry

    lax.fori_loop(0, rows // 16, step, 0)
    keep_ref[...] = t_ref[0:8]
    send_ref[...] = t_ref[8:16].astype(BF16)


def split_taps(t_ref, got_ref, k0, k3, send):
    n = k0.shape[0]
    for ref, at in ((k0, 0), (send, n), (k3, 3 * n)):
        m = ref.shape[0]
        ref[...] = (t_ref[at : at + m] + got_ref[at : at + m].astype(F32)).astype(ref.dtype)


def middle_taps(k0, k3, got, keep, send):
    n = k0.shape[0]
    keep[...] = k0[...] + got[0:n].astype(F32)
    send[...] = (k3[...] + got[n:].astype(F32)).astype(BF16)


def sum_pieces(k, *refs):
    parts, keep, send = refs[:-2], refs[-2], refs[-1]
    for ref, i in ((keep, 0), (send, 1)):
        total = k[i].astype(F32)
        for r in parts:
            total = total + r[i].astype(F32)
        ref[...] = total.astype(ref.dtype)


def finish_rows(keep, got, o_ref, *, scale):
    o_ref[...] = (keep[...] + got[...].astype(F32)) * scale


def finish_taps(pos_ref, reach_ref, part_ref, got, t_ref, *, scale):
    f = part_ref[...] + got[...].astype(F32)
    chan = pos_ref[0] * 2 + pos_ref[1]
    place = pos_ref[4]
    own_cols = iota((16, 8, 256), 1) == (iota((16, 8, 256), 2) & 7)
    first = chan * 128 // GROUP
    limit = jnp.where(iota((VN, 128), 1) < GROUP, reach_ref[first], reach_ref[first + 1])
    inside = place * VN + iota((VN, 128), 0) < limit
    for d in range(2):
        v = iota((VN, 256), 1) >> 3
        e = (iota((VN, 256), 0) == (v if d == 0 else (VN - 1) - v)).astype(BF16)
        part = f[16 * d : 16 * d + 16, :]
        spread = jnp.broadcast_to(part[:, None, :], (16, 8, 256))
        spread = jnp.where(own_cols, spread, 0.0).reshape(128, 256)
        high = spread.astype(BF16)
        low = (spread - high.astype(F32)).astype(BF16)
        t_ref[d] = jnp.where(inside, (dot(e, high, NT) + dot(e, low, NT)) * scale, 0.0)


def swap(v, axis, mask):
    return lax.ppermute(v, axis, [(i, i ^ mask) for i in range(lax.axis_size(axis))])


def smem():
    return pl.BlockSpec(memory_space=pltpu.SMEM)


def call(body, out_shape, args, scalars=1, scratch=(), limit=16, held_in=pltpu.VMEM):
    vmem = pl.BlockSpec(memory_space=pltpu.VMEM)
    where = pl.BlockSpec(memory_space=held_in)
    held = [pltpu.with_memory_space_constraint(a, held_in) for a in args[scalars:]]
    return pl.pallas_call(
        body,
        out_shape=out_shape,
        in_specs=[smem()] * scalars + [where] * len(held),
        out_specs=jax.tree.map(lambda _: vmem, out_shape),
        scratch_shapes=list(scratch),
        compiler_params=pltpu.CompilerParams(vmem_limit_bytes=limit << 20),
    )(*args[:scalars], *held)


def on_device_0(out_grad, out_weight, conv_input, gate_values, conv_output, filters, filter_reach):
    shape = jax.ShapeDtypeStruct
    rows, tok = conv_input.shape
    feats = out_grad.shape[1]
    seq_count = lax.axis_size("seq")
    place = lax.axis_index("seq").astype(jnp.int32)
    chan = lax.axis_index("chan").astype(jnp.int32)
    pos = jnp.stack([chan >> 1, chan & 1, place >> 3, (place >> 1) & 3, place])
    half = rows // 2
    scale = 1.0 / float(tok * seq_count) ** 0.5

    mine, other = call(
        gate_rows,
        [shape((half, tok), BF16)] * 2,
        (pos, conv_output, gate_values),
        scratch=[pltpu.VMEM((rows, tok), BF16)] * 2 + [pltpu.SemaphoreType.DMA((2,))],
        held_in=pltpu.HBM,
    )
    own = jnp.concatenate([mine, swap(other, "seq", 1)], axis=1)
    og_core = swap(out_grad, "seq", 1)
    rx = swap(own, "chan", 1)
    own1 = swap(own, "chan", 2)
    rx3 = swap(rx, "chan", 6)
    owns = swap(jnp.stack([own, own1]), "chan", 6)
    rxs = swap(jnp.stack([rx, rx3]), "chan", 2)

    keep, send = call(
        first_product,
        [shape((rows * 4, tok), BF16)] * 2,
        (pos, out_weight, out_grad),
        scratch=[
            pltpu.VMEM((4, 2 * rows, feats), BF16),
            pltpu.VMEM((tok, feats), BF16),
            pltpu.SemaphoreType.DMA((9,)),
        ],
        held_in=pltpu.HBM,
    )
    keep, s1, s3, s2 = call(
        middle_sums,
        [shape((rows, tok), F32)] + [shape((rows, tok), BF16)] * 3,
        (keep, swap(send, "chan", 1)),
        scalars=0,
    )
    s1, s3, s2 = swap(s1, "chan", 2), swap(s3, "chan", 6), swap(s2, "chan", 4)
    grad_gate, grad_conv = call(
        gate_grads,
        [shape((rows, tok), F32), shape((rows, tok), BF16)],
        (keep, s1, s3, s2, conv_output, gate_values),
        scalars=0,
    )

    halo_core = swap(grad_conv, "seq", 1)
    pairs = [(i, i + 1) for i in range(1, seq_count - 1, 2)]
    halo_out = lax.ppermute(grad_conv, "seq", pairs + [(b, a) for a, b in pairs])

    e = call(
        second_product,
        [shape((2, half, feats), BF16)] * 4,
        (pos, own, rx, own1, rx3, owns, rxs, out_grad, og_core),
        scratch=[pltpu.VMEM((8, half, 2 * tok), BF16)],
    )
    e = [e[0], swap(e[1], "seq", 2), swap(e[2], "seq", 6), swap(e[3], "seq", 4)]

    groups = rows // 8
    prepared = call(
        prepare,
        [
            shape((groups, 2, 128, 256), BF16),
            shape((groups, 256, tok), BF16),
            shape((groups, 256, tok), BF16),
        ],
        (pos, filter_reach, filters, conv_input),
        scalars=2,
    )
    grad_input, tap_keep, tap_send = call(
        conv_grads,
        [
            shape((rows, tok), F32),
            shape((8, rows // 4, 256), F32),
            shape((8, rows // 4, 256), BF16),
        ],
        (pos, grad_conv, halo_core, halo_out, *prepared),
        scratch=[
            pltpu.VMEM((2, 256, 3 * tok), BF16),
            pltpu.VMEM((16, rows // 4, 256), F32),
        ],
    )
    f_got = swap(tap_send, "seq", 1)
    piece = (2, rows // 4, 256)
    f0, f3, f_send = call(
        split_taps,
        [shape(piece, F32)] * 2 + [shape((4,) + piece[1:], BF16)],
        (tap_keep, f_got),
        scalars=0,
    )
    f0, f_send = call(
        middle_taps,
        [shape(piece, F32), shape(piece, BF16)],
        (f0, f3, swap(f_send, "seq", 2)),
        scalars=0,
    )
    f = [f0, swap(f_send, "seq", 6)]
    e_keep, e_send = call(
        sum_pieces, [shape((half, feats), F32), shape((half, feats), BF16)], e, scalars=0
    )
    e_got = swap(e_send, "seq", 8)
    f_keep, f_send = call(sum_pieces, [shape(piece[1:], F32), shape(piece[1:], BF16)], f, scalars=0)
    f_got = swap(f_send, "seq", 8)
    grad_weight = call(
        functools.partial(finish_rows, scale=scale),
        shape((half, feats), F32),
        (e_keep, e_got),
        scalars=0,
    )
    grad_filters = call(
        functools.partial(finish_taps, scale=scale),
        shape((2, VN, rows), F32),
        (pos, filter_reach, f_keep, f_got),
        scalars=2,
    )
    return (grad_input, grad_gate, grad_weight, jnp.transpose(grad_filters, (0, 2, 1)))


def solution(mesh):
    return jax.shard_map(
        on_device_0,
        mesh=mesh,
        in_specs=(
            P("seq", "chan"),
            P(None, "chan"),
            P("chan", "seq"),
            P("chan", "seq"),
            P("chan", "seq"),
            P(None, "chan", None),
            P(),
        ),
        out_specs=(P("chan", "seq"), P("chan", "seq"), P("seq", "chan"), P(None, "chan", "seq")),
        check_vma=False,
    )
```

```python
import functools

import jax
import jax.numpy as jnp
from jax import lax
from jax.experimental import pallas as pl
from jax.experimental.pallas import tpu as pltpu
from jax.sharding import PartitionSpec as P


GROUP = 64
VN = 32
F32 = jnp.float32
BF16 = jnp.bfloat16


def iota(shape, dim):
    return lax.broadcasted_iota(jnp.int32, shape, dim)


def dot(a, b, dims=(((1,), (0,)), ((), ()))):
    return lax.dot_general(a, b, dims, preferred_element_type=F32)


NT = (((1,), (1,)), ((), ()))


RELS = (0, 1, 3, 2)


def gate_rows(pos_ref, v_hbm, g_hbm, mine, other, v_ref, g_ref, sems):
    loads = [
        pltpu.make_async_copy(v_hbm, v_ref, sems.at[0]),
        pltpu.make_async_copy(g_hbm, g_ref, sems.at[1]),
    ]
    for load in loads:
        load.start()
    for load in loads:
        load.wait()
    half = mine.shape[0]
    core = pos_ref[4] & 1
    for ref, part in ((mine, core), (other, 1 - core)):
        band = pl.ds(pl.multiple_of(part * half, half), half)
        ref[...] = (v_ref[band, :].astype(F32) * g_ref[band, :].astype(F32)).astype(BF16)


def first_product(pos_ref, w_hbm, og_hbm, keep, send, w_ref, og_ref, sems):
    z = pos_ref[0]
    x = pos_ref[1]
    og_load = pltpu.make_async_copy(og_hbm, og_ref, sems.at[8])
    og_load.start()
    loads = []
    for i, rel in enumerate(RELS):
        for a in range(2):
            rows = pl.ds(pl.multiple_of(((z ^ rel) * 2 + (x ^ a)) * 128, 128), 128)
            part = w_ref.at[i, 128 * a : 128 * (a + 1)]
            loads.append(pltpu.make_async_copy(w_hbm.at[rows], part, sems.at[2 * i + a]))
            loads[-1].start()
    og_load.wait()
    og = og_ref[...]
    for i in range(4):
        loads[2 * i].wait()
        loads[2 * i + 1].wait()
        p = dot(w_ref[i], og, NT).astype(BF16)
        keep[128 * i : 128 * (i + 1), :] = p[:128]
        send[128 * i : 128 * (i + 1), :] = p[128:]


def middle_sums(k_ref, r_ref, *outs):
    n = k_ref.shape[0] // 4
    for i, ref in enumerate(outs):
        band = slice(n * i, n * i + n)
        ref[...] = (k_ref[band, :].astype(F32) + r_ref[band, :].astype(F32)).astype(ref.dtype)


def gate_grads(k_ref, r1, r3, r2, v_ref, g_ref, gate_ref, conv_ref):
    total = k_ref[...] + r1[...].astype(F32) + r3[...].astype(F32) + r2[...].astype(F32)
    gate_ref[...] = total * v_ref[...].astype(F32)
    conv_ref[...] = (total * g_ref[...].astype(F32)).astype(BF16)


def second_product(pos_ref, b0, b1, b3, b2, og_ref, ogs_ref, *refs):
    outs, g_ref = refs[:4], refs[4]
    for i, ref in enumerate((b0, b1, b2, b3)):
        g_ref[i] = ref[0]
        g_ref[4 + i] = ref[1]
    z = pos_ref[0]
    x = pos_ref[1]
    xh = pos_ref[2]
    y = pos_ref[3]
    tok = og_ref.shape[0]
    for ref, rel in zip(outs, RELS):
        for a in range(2):
            j = (xh ^ a) * 4 + (y ^ rel)
            g = g_ref[((j % 2) ^ x) * 4 + ((j // 2) ^ z)]
            ref[a] = (dot(g[:, :tok], og_ref[...]) + dot(g[:, tok:], ogs_ref[...])).astype(BF16)


def lagged(x, shifts, width):
    pair = [pltpu.roll(x, s % width, 1) if s % width else x for s in shifts]
    return jnp.concatenate(pair, axis=0).astype(BF16)


def prepare(pos_ref, reach_ref, f_ref, x_ref, l_ref, ui_ref, uo_ref):
    rows, n = x_ref.shape
    width = 3 * n
    chan = pos_ref[0] * 2 + pos_ref[1]
    own_rows = (iota((128, 256), 0) & 7) == (iota((128, 256), 1) & 7)
    ef = (iota((128, 256), 0) == (iota((128, 256), 1) >> 3)).astype(BF16)
    eb = (iota((128, 256), 0) == (VN - 1) - (iota((128, 256), 1) >> 3)).astype(BF16)
    taps = f_ref.shape[2]
    lag = iota((8, taps), 1)

    def step(i, carry):
        base = pl.multiple_of(i * 16, 16)
        band = pl.ds(base, 16)
        own16 = x_ref[band, :].astype(F32)
        filt16 = [f_ref[d, band, :].astype(F32) for d in range(2)]
        inside = lag < reach_ref[(chan * rows + base) // GROUP]
        zero = jnp.zeros((8, n), F32)
        for h in range(2):
            group = 2 * i + h
            for d, e in ((0, ef), (1, eb)):
                f8 = jnp.where(inside, filt16[d][8 * h : 8 * h + 8], 0.0)
                rolled = [f8 if b == 0 else pltpu.roll(f8, taps - 32 * b, 1) for b in range(4)]
                cut = [rolled[u % 4][:, 128 * (u // 4) : 128 * (u // 4) + 128] for u in range(16)]
                spread = dot(jnp.concatenate(cut, axis=0).astype(BF16), e)
                l_ref[group, d] = jnp.where(own_rows, spread, 0.0).astype(BF16)
            own = jnp.concatenate([zero, own16[8 * h : 8 * h + 8], zero], axis=1)
            bases = (
                (lagged(own, (0, 32), width), lagged(own, (64, 96), width)),
                (lagged(own, (-32, -64), width), lagged(own, (-96, -128), width)),
            )
            for d in range(2):
                for k in range(8):
                    start = n - 128 * (k // 2) if d == 0 else 128 * (k // 2)
                    part = bases[d][k % 2][:, start : start + 2 * n]
                    inner, outer = (part[:, :n], part[:, n:]) if d == 0 else (part[:, n:], part[:, :n])
                    at = 128 * d + 16 * k
                    ui_ref[group, at : at + 16, :] = inner
                    uo_ref[group, at : at + 16, :] = outer
        return carry

    lax.fori_loop(0, rows // 16, step, 0)


def with_halos(pos_ref, gm_ref, gs_ref, gp_ref, band):
    core0 = (pos_ref[4] & 1) == 0
    gm = gm_ref[band, :].astype(F32)
    gs = gs_ref[band, :].astype(F32)
    gp = gp_ref[band, :].astype(F32)
    return jnp.concatenate([jnp.where(core0, gp, gs), gm, jnp.where(core0, gs, gp)], axis=1)


def fill_shifted(h_ref, h, ext):
    width = ext.shape[1]
    two = jnp.concatenate([ext, pltpu.roll(ext, width - 1, 1)], axis=0).astype(BF16)
    for k in range(VN // 2):
        moved = two if k == 0 else pltpu.roll(two, width - 2 * k, 1)
        h_ref[h, 16 * k : 16 * k + 16, :] = moved


def tap_grads(pos_ref, gm_ref, gs_ref, gp_ref, ui_ref, uo_ref, t_ref, h_ref, acc_ref):
    rows, n = gm_ref.shape
    own_cols = iota((16, 8, 256), 1) == (iota((16, 8, 256), 2) & 7)

    def step(i, carry):
        band = pl.ds(pl.multiple_of(i * 16, 16), 16)
        ext16 = with_halos(pos_ref, gm_ref, gs_ref, gp_ref, band)
        for h in range(2):
            group = 2 * i + h
            fill_shifted(h_ref, h, ext16[8 * h : 8 * h + 8])
            inner = dot(ui_ref[group], h_ref[h, :, n : 2 * n], NT)
            for d in range(2):
                start = 2 * n * (1 - d)
                cross = inner[128 * d : 128 * d + 128] + dot(
                    uo_ref[group, 128 * d : 128 * d + 128, :], h_ref[h, :, start : start + n], NT
                )
                sums = jnp.sum(jnp.where(own_cols, cross.reshape(16, 8, 256), 0.0), axis=1)
                row = d * (rows // 8) + group
                for u in range(16):
                    acc_ref[u, pl.ds(row, 1), :] = sums[u : u + 1]
        return carry

    lax.fori_loop(0, rows // 16, step, 0)
    t_ref[...] = acc_ref[...].astype(BF16)


def input_grad(pos_ref, gm_ref, gs_ref, gp_ref, l_ref, o_ref, h_ref):
    rows, n = gm_ref.shape
    lanes = n // 128

    def step(i, carry):
        band = pl.ds(pl.multiple_of(i * 16, 16), 16)
        ext16 = with_halos(pos_ref, gm_ref, gs_ref, gp_ref, band)
        outs = []
        for h in range(2):
            group = 2 * i + h
            fill_shifted(h_ref, h, ext16[8 * h : 8 * h + 8])
            total = None
            for d in range(2):
                acc = [[None] * (lanes + (b > 0)) for b in range(4)]
                for j in range(lanes):
                    if d == 0:
                        lo, hi = (0, 64) if j == 0 else (64, 128) if j == lanes - 1 else (0, 128)
                    else:
                        lo, hi = (48, 128) if j == 0 else (0, 64) if j == lanes - 1 else (0, 128)
                    at = n * (1 - d) + 256 * j
                    p = dot(l_ref[group, d, lo:hi, :], h_ref[h, :, at : at + 256])
                    for u in range(lo // 8, hi // 8):
                        a, b = divmod(u + d, 4)
                        for c in range(2):
                            q = 2 * j + c
                            slot = q - a if d == 0 else q - (lanes - (b > 0)) + a
                            if 0 <= slot < len(acc[b]):
                                part = p[8 * u - lo : 8 * u - lo + 8, 128 * c : 128 * c + 128]
                                acc[b][slot] = part if acc[b][slot] is None else acc[b][slot] + part
                for b in range(4):
                    line = jnp.concatenate(acc[b], axis=1)
                    if b and d == 0:
                        line = pltpu.roll(line, n + 128 - 32 * b, 1)[:, :n]
                    elif b:
                        line = pltpu.roll(line, 32 * b, 1)[:, 128:]
                    total = line if total is None else total + line
            outs.append(total)
        o_ref[band, :] = jnp.concatenate(outs, axis=0)
        return carry

    lax.fori_loop(0, rows // 16, step, 0)


def sum_pieces(k, r1, r3, r2, keep, send):
    for ref, i in ((keep, 0), (send, 1)):
        total = k[i].astype(F32)
        for r in (r1, r3, r2):
            total = total + r[i].astype(F32)
        ref[...] = total.astype(ref.dtype)


def finish_rows(keep, got, o_ref, *, scale):
    o_ref[...] = (keep[...] + got[...].astype(F32)) * scale


def finish_taps(pos_ref, reach_ref, got, t_ref, *, scale):
    f = got[0].astype(F32)
    for i in range(1, got.shape[0]):
        f = f + got[i].astype(F32)
    chan = pos_ref[0] * 2 + pos_ref[1]
    place = pos_ref[4]
    own_cols = iota((16, 8, 256), 1) == (iota((16, 8, 256), 2) & 7)
    first = chan * 128 // GROUP
    limit = jnp.where(iota((VN, 128), 1) < GROUP, reach_ref[first], reach_ref[first + 1])
    inside = place * VN + iota((VN, 128), 0) < limit
    for d in range(2):
        v = iota((VN, 256), 1) >> 3
        e = (iota((VN, 256), 0) == (v if d == 0 else (VN - 1) - v)).astype(BF16)
        part = f[16 * d : 16 * d + 16, :]
        spread = jnp.broadcast_to(part[:, None, :], (16, 8, 256))
        spread = jnp.where(own_cols, spread, 0.0).reshape(128, 256)
        high = spread.astype(BF16)
        low = (spread - high.astype(F32)).astype(BF16)
        t_ref[d] = jnp.where(inside, (dot(e, high, NT) + dot(e, low, NT)) * scale, 0.0)


def swap(v, axis, mask):
    return lax.ppermute(v, axis, [(i, i ^ mask) for i in range(lax.axis_size(axis))])


def smem():
    return pl.BlockSpec(memory_space=pltpu.SMEM)


def call(body, out_shape, args, scalars=1, scratch=(), limit=16, held_in=pltpu.VMEM):
    vmem = pl.BlockSpec(memory_space=pltpu.VMEM)
    where = pl.BlockSpec(memory_space=held_in)
    held = [pltpu.with_memory_space_constraint(a, held_in) for a in args[scalars:]]
    return pl.pallas_call(
        body,
        out_shape=out_shape,
        in_specs=[smem()] * scalars + [where] * len(held),
        out_specs=jax.tree.map(lambda _: vmem, out_shape),
        scratch_shapes=list(scratch),
        compiler_params=pltpu.CompilerParams(vmem_limit_bytes=limit << 20),
    )(*args[:scalars], *held)


def on_device_0(out_grad, out_weight, conv_input, gate_values, conv_output, filters, filter_reach):
    shape = jax.ShapeDtypeStruct
    rows, tok = conv_input.shape
    feats = out_grad.shape[1]
    seq_count = lax.axis_size("seq")
    place = lax.axis_index("seq").astype(jnp.int32)
    chan = lax.axis_index("chan").astype(jnp.int32)
    pos = jnp.stack([chan >> 1, chan & 1, place >> 3, (place >> 1) & 3, place])
    half = rows // 2
    scale = 1.0 / float(tok * seq_count) ** 0.5

    mine, other = call(
        gate_rows,
        [shape((half, tok), BF16)] * 2,
        (pos, conv_output, gate_values),
        scratch=[pltpu.VMEM((rows, tok), BF16)] * 2 + [pltpu.SemaphoreType.DMA((2,))],
        held_in=pltpu.HBM,
    )
    own = jnp.concatenate([mine, swap(other, "seq", 1)], axis=1)
    og_core = swap(out_grad, "seq", 1)
    pair = jnp.stack([own, swap(own, "chan", 1)])
    b1 = swap(pair, "chan", 2)
    b3 = swap(pair, "chan", 6)
    b2 = swap(pair, "chan", 4)

    keep, send = call(
        first_product,
        [shape((rows * 4, tok), BF16)] * 2,
        (pos, out_weight, out_grad),
        scratch=[
            pltpu.VMEM((4, 2 * rows, feats), BF16),
            pltpu.VMEM((tok, feats), BF16),
            pltpu.SemaphoreType.DMA((9,)),
        ],
        held_in=pltpu.HBM,
    )
    keep, s1, s3, s2 = call(
        middle_sums,
        [shape((rows, tok), F32)] + [shape((rows, tok), BF16)] * 3,
        (keep, swap(send, "chan", 1)),
        scalars=0,
    )
    s1, s3, s2 = swap(s1, "chan", 2), swap(s3, "chan", 6), swap(s2, "chan", 4)
    grad_gate, grad_conv = call(
        gate_grads,
        [shape((rows, tok), F32), shape((rows, tok), BF16)],
        (keep, s1, s3, s2, conv_output, gate_values),
        scalars=0,
    )

    halo_core = swap(grad_conv, "seq", 1)
    pairs = [(i, i + 1) for i in range(1, seq_count - 1, 2)]
    halo_out = lax.ppermute(grad_conv, "seq", pairs + [(b, a) for a, b in pairs])

    e = call(
        second_product,
        [shape((2, half, feats), BF16)] * 4,
        (pos, pair, b1, b3, b2, out_grad, og_core),
        scratch=[pltpu.VMEM((8, half, 2 * tok), BF16)],
    )
    e = [e[0], swap(e[1], "seq", 2), swap(e[2], "seq", 6), swap(e[3], "seq", 4)]

    groups = rows // 8
    prepared = call(
        prepare,
        [
            shape((groups, 2, 128, 256), BF16),
            shape((groups, 256, tok), BF16),
            shape((groups, 256, tok), BF16),
        ],
        (pos, filter_reach, filters, conv_input),
        scalars=2,
    )
    halos = (pos, grad_conv, halo_core, halo_out)
    shifted = pltpu.VMEM((2, 256, 3 * tok), BF16)
    tap_sums = call(
        tap_grads,
        shape((seq_count, rows // 4, 256), BF16),
        (*halos, *prepared[1:]),
        scratch=[shifted, pltpu.VMEM((seq_count, rows // 4, 256), F32)],
    )
    tap_sums = lax.all_to_all(tap_sums, "seq", 0, 0)
    grad_input = call(input_grad, shape((rows, tok), F32), (*halos, prepared[0]), scratch=[shifted])
    e_keep, e_send = call(
        sum_pieces, [shape((half, feats), F32), shape((half, feats), BF16)], e, scalars=0
    )
    e_got = swap(e_send, "seq", 8)
    grad_weight = call(
        functools.partial(finish_rows, scale=scale),
        shape((half, feats), F32),
        (e_keep, e_got),
        scalars=0,
    )
    grad_filters = call(
        functools.partial(finish_taps, scale=scale),
        shape((2, VN, rows), F32),
        (pos, filter_reach, tap_sums),
        scalars=2,
    )
    return (grad_input, grad_gate, grad_weight, jnp.transpose(grad_filters, (0, 2, 1)))


def solution(mesh):
    return jax.shard_map(
        on_device_0,
        mesh=mesh,
        in_specs=(
            P("seq", "chan"),
            P(None, "chan"),
            P("chan", "seq"),
            P("chan", "seq"),
            P("chan", "seq"),
            P(None, "chan", None),
            P(),
        ),
        out_specs=(P("chan", "seq"), P("chan", "seq"), P("seq", "chan"), P(None, "chan", "seq")),
        check_vma=False,
    )
```

```python
import functools

import jax
import jax.numpy as jnp
from jax import lax
from jax.experimental import pallas as pl
from jax.experimental.pallas import tpu as pltpu
from jax.sharding import PartitionSpec as P


GROUP = 64
VN = 32
F32 = jnp.float32
BF16 = jnp.bfloat16


def iota(shape, dim):
    return lax.broadcasted_iota(jnp.int32, shape, dim)


def dot(a, b, dims=(((1,), (0,)), ((), ()))):
    return lax.dot_general(a, b, dims, preferred_element_type=F32)


NT = (((1,), (1,)), ((), ()))


RELS = (0, 1, 3, 2)


def gate_rows(pos_ref, v_hbm, g_hbm, mine, other, v_ref, g_ref, sems):
    loads = [
        pltpu.make_async_copy(v_hbm, v_ref, sems.at[0]),
        pltpu.make_async_copy(g_hbm, g_ref, sems.at[1]),
    ]
    for load in loads:
        load.start()
    for load in loads:
        load.wait()
    half = mine.shape[0]
    core = pos_ref[4] & 1
    for ref, part in ((mine, core), (other, 1 - core)):
        band = pl.ds(pl.multiple_of(part * half, half), half)
        ref[...] = (v_ref[band, :].astype(F32) * g_ref[band, :].astype(F32)).astype(BF16)


def first_product(pos_ref, w_hbm, og_hbm, keep, send, w_ref, og_ref, sems):
    z = pos_ref[0]
    x = pos_ref[1]
    og_load = pltpu.make_async_copy(og_hbm, og_ref, sems.at[8])
    og_load.start()
    loads = []
    for i, rel in enumerate(RELS):
        for a in range(2):
            rows = pl.ds(pl.multiple_of(((z ^ rel) * 2 + (x ^ a)) * 128, 128), 128)
            part = w_ref.at[i, 128 * a : 128 * (a + 1)]
            loads.append(pltpu.make_async_copy(w_hbm.at[rows], part, sems.at[2 * i + a]))
            loads[-1].start()
    og_load.wait()
    og = og_ref[...]
    for i in range(4):
        loads[2 * i].wait()
        loads[2 * i + 1].wait()
        p = dot(w_ref[i], og, NT).astype(BF16)
        keep[128 * i : 128 * (i + 1), :] = p[:128]
        send[128 * i : 128 * (i + 1), :] = p[128:]


def middle_sums(k_ref, r_ref, *outs):
    n = k_ref.shape[0] // 4
    for i, ref in enumerate(outs):
        band = slice(n * i, n * i + n)
        ref[...] = (k_ref[band, :].astype(F32) + r_ref[band, :].astype(F32)).astype(ref.dtype)


def gate_grads(k_ref, r1, r3, r2, v_ref, g_ref, gate_ref, conv_ref):
    total = k_ref[...] + r1[...].astype(F32) + r3[...].astype(F32) + r2[...].astype(F32)
    gate_ref[...] = total * v_ref[...].astype(F32)
    conv_ref[...] = (total * g_ref[...].astype(F32)).astype(BF16)


def second_product(pos_ref, b0, b1, b3, b2, og_ref, ogs_ref, *refs):
    outs, g_ref = refs[:4], refs[4]
    for i, ref in enumerate((b0, b1, b2, b3)):
        g_ref[i] = ref[0]
        g_ref[4 + i] = ref[1]
    z = pos_ref[0]
    x = pos_ref[1]
    xh = pos_ref[2]
    y = pos_ref[3]
    tok = og_ref.shape[0]
    for ref, rel in zip(outs, RELS):
        for a in range(2):
            j = (xh ^ a) * 4 + (y ^ rel)
            g = g_ref[((j % 2) ^ x) * 4 + ((j // 2) ^ z)]
            ref[a] = (dot(g[:, :tok], og_ref[...]) + dot(g[:, tok:], ogs_ref[...])).astype(BF16)


def lagged(x, shifts, width):
    pair = [pltpu.roll(x, s % width, 1) if s % width else x for s in shifts]
    return jnp.concatenate(pair, axis=0).astype(BF16)


def prepare(pos_ref, reach_ref, f_ref, x_ref, l_ref, u_ref):
    rows, n = x_ref.shape
    width = 3 * n
    chan = pos_ref[0] * 2 + pos_ref[1]
    own_rows = (iota((128, 256), 0) & 7) == (iota((128, 256), 1) & 7)
    ef = (iota((128, 256), 0) == (iota((128, 256), 1) >> 3)).astype(BF16)
    eb = (iota((128, 256), 0) == (VN - 1) - (iota((128, 256), 1) >> 3)).astype(BF16)
    taps = f_ref.shape[2]
    lag = iota((8, taps), 1)

    def step(i, carry):
        base = pl.multiple_of(i * 16, 16)
        band = pl.ds(base, 16)
        own16 = x_ref[band, :].astype(F32)
        filt16 = [f_ref[d, band, :].astype(F32) for d in range(2)]
        inside = lag < reach_ref[(chan * rows + base) // GROUP]
        zero = jnp.zeros((8, n), F32)
        for h in range(2):
            group = 2 * i + h
            for d, e in ((0, ef), (1, eb)):
                f8 = jnp.where(inside, filt16[d][8 * h : 8 * h + 8], 0.0)
                rolled = [f8 if b == 0 else pltpu.roll(f8, taps - 32 * b, 1) for b in range(4)]
                cut = [rolled[u % 4][:, 128 * (u // 4) : 128 * (u // 4) + 128] for u in range(16)]
                spread = dot(jnp.concatenate(cut, axis=0).astype(BF16), e)
                l_ref[group, d] = jnp.where(own_rows, spread, 0.0).astype(BF16)
            own = jnp.concatenate([zero, own16[8 * h : 8 * h + 8], zero], axis=1)
            bases = (
                (lagged(own, (0, 32), width), lagged(own, (64, 96), width)),
                (lagged(own, (-32, -64), width), lagged(own, (-96, -128), width)),
            )
            for d in range(2):
                for k in range(8):
                    start = n - 128 * (k // 2) if d == 0 else 128 * (k // 2)
                    u_ref[group, d, 16 * k : 16 * k + 16, :] = bases[d][k % 2][:, start : start + 2 * n]
        return carry

    lax.fori_loop(0, rows // 16, step, 0)


def fill_shifted(h_ref, h, ext):
    width = ext.shape[1]
    two = jnp.concatenate([ext, pltpu.roll(ext, width - 1, 1)], axis=0).astype(BF16)
    for k in range(VN // 2):
        moved = two if k == 0 else pltpu.roll(two, width - 2 * k, 1)
        h_ref[h, 16 * k : 16 * k + 16, :] = moved


def input_part(d, l_ref, h_ref, group, h):
    n = h_ref.shape[2] // 2
    lanes = n // 128
    total = None
    acc = [[None] * (lanes + (b > 0)) for b in range(4)]
    for j in range(lanes):
        if d == 0:
            lo, hi = (0, 64) if j == 0 else (64, 128) if j == lanes - 1 else (0, 128)
        else:
            lo, hi = (48, 128) if j == 0 else (0, 64) if j == lanes - 1 else (0, 128)
        p = dot(l_ref[group, d, lo:hi, :], h_ref[h, :, 256 * j : 256 * j + 256])
        for u in range(lo // 8, hi // 8):
            a, b = divmod(u + d, 4)
            for c in range(2):
                q = 2 * j + c
                slot = q - a if d == 0 else q - (lanes - (b > 0)) + a
                if 0 <= slot < len(acc[b]):
                    part = p[8 * u - lo : 8 * u - lo + 8, 128 * c : 128 * c + 128]
                    acc[b][slot] = part if acc[b][slot] is None else acc[b][slot] + part
    for b in range(4):
        line = jnp.concatenate(acc[b], axis=1)
        if b and d == 0:
            line = pltpu.roll(line, n + 128 - 32 * b, 1)[:, :n]
        elif b:
            line = pltpu.roll(line, 32 * b, 1)[:, 128:]
        total = line if total is None else total + line
    return total


def tap_part(d, u_ref, h_ref, group, h, own_cols, acc_ref):
    cross = dot(u_ref[group, d], h_ref[h], NT)
    sums = jnp.sum(jnp.where(own_cols, cross.reshape(16, 8, 256), 0.0), axis=1)
    for u in range(16):
        acc_ref[u, pl.ds(group, 1), :] = sums[u : u + 1]


def one_side(pos_ref, gm_ref, halo_ref, h_ref, per_group, outer):
    core = pos_ref[4] & 1
    for c in range(2):
        d = 1 - c if outer else c

        @pl.when(core == c)
        def _():
            def step(i, carry):
                band = pl.ds(pl.multiple_of(i * 16, 16), 16)
                gm = gm_ref[band, :].astype(F32)
                halo = halo_ref[band, :].astype(F32)
                ext16 = jnp.concatenate([gm, halo] if d == 0 else [halo, gm], axis=1)
                for h in range(2):
                    fill_shifted(h_ref, h, ext16[8 * h : 8 * h + 8])
                per_group(d, i, band)
                return carry

            lax.fori_loop(0, gm_ref.shape[0] // 16, step, 0)


def inner_side(pos_ref, gm_ref, halo_ref, l_ref, u_ref, o_ref, t_ref, h_ref, acc_ref):
    own_cols = iota((16, 8, 256), 1) == (iota((16, 8, 256), 2) & 7)

    def per_group(d, i, band):
        o_ref[band, :] = jnp.concatenate(
            [input_part(d, l_ref, h_ref, 2 * i + h, h) for h in range(2)], axis=0
        )
        for h in range(2):
            tap_part(d, u_ref, h_ref, 2 * i + h, h, own_cols, acc_ref)

    one_side(pos_ref, gm_ref, halo_ref, h_ref, per_group, False)
    t_ref[...] = acc_ref[...].astype(BF16)


def outer_taps(pos_ref, gm_ref, halo_ref, u_ref, inner_ref, t_ref, h_ref, acc_ref):
    own_cols = iota((16, 8, 256), 1) == (iota((16, 8, 256), 2) & 7)

    def per_group(d, i, band):
        for h in range(2):
            tap_part(d, u_ref, h_ref, 2 * i + h, h, own_cols, acc_ref)

    one_side(pos_ref, gm_ref, halo_ref, h_ref, per_group, True)
    count = inner_ref.shape[1]
    core = pos_ref[4] & 1
    for c in range(2):

        @pl.when(core == c)
        def _():
            t_ref[:, count * c : count * c + count, :] = inner_ref[...]
            t_ref[:, count * (1 - c) : count * (1 - c) + count, :] = acc_ref[...].astype(BF16)


def outer_input(pos_ref, gm_ref, halo_ref, l_ref, inner_ref, o_ref, h_ref):
    def per_group(d, i, band):
        parts = [input_part(d, l_ref, h_ref, 2 * i + h, h) for h in range(2)]
        o_ref[band, :] = inner_ref[band, :] + jnp.concatenate(parts, axis=0)

    one_side(pos_ref, gm_ref, halo_ref, h_ref, per_group, True)


def sum_pieces(k, r1, r3, r2, keep, send):
    for ref, i in ((keep, 0), (send, 1)):
        total = k[i].astype(F32)
        for r in (r1, r3, r2):
            total = total + r[i].astype(F32)
        ref[...] = total.astype(ref.dtype)


def finish_rows(keep, got, o_ref, *, scale):
    o_ref[...] = (keep[...] + got[...].astype(F32)) * scale


def finish_taps(pos_ref, reach_ref, got, t_ref, *, scale):
    f = got[0].astype(F32)
    for i in range(1, got.shape[0]):
        f = f + got[i].astype(F32)
    chan = pos_ref[0] * 2 + pos_ref[1]
    place = pos_ref[4]
    own_cols = iota((16, 8, 256), 1) == (iota((16, 8, 256), 2) & 7)
    first = chan * 128 // GROUP
    limit = jnp.where(iota((VN, 128), 1) < GROUP, reach_ref[first], reach_ref[first + 1])
    inside = place * VN + iota((VN, 128), 0) < limit
    for d in range(2):
        v = iota((VN, 256), 1) >> 3
        e = (iota((VN, 256), 0) == (v if d == 0 else (VN - 1) - v)).astype(BF16)
        part = f[16 * d : 16 * d + 16, :]
        spread = jnp.broadcast_to(part[:, None, :], (16, 8, 256))
        spread = jnp.where(own_cols, spread, 0.0).reshape(128, 256)
        high = spread.astype(BF16)
        low = (spread - high.astype(F32)).astype(BF16)
        t_ref[d] = jnp.where(inside, (dot(e, high, NT) + dot(e, low, NT)) * scale, 0.0)


def swap(v, axis, mask):
    return lax.ppermute(v, axis, [(i, i ^ mask) for i in range(lax.axis_size(axis))])


def smem():
    return pl.BlockSpec(memory_space=pltpu.SMEM)


def call(body, out_shape, args, scalars=1, scratch=(), limit=16, held_in=pltpu.VMEM):
    vmem = pl.BlockSpec(memory_space=pltpu.VMEM)
    where = pl.BlockSpec(memory_space=held_in)
    held = [pltpu.with_memory_space_constraint(a, held_in) for a in args[scalars:]]
    return pl.pallas_call(
        body,
        out_shape=out_shape,
        in_specs=[smem()] * scalars + [where] * len(held),
        out_specs=jax.tree.map(lambda _: vmem, out_shape),
        scratch_shapes=list(scratch),
        compiler_params=pltpu.CompilerParams(vmem_limit_bytes=limit << 20),
    )(*args[:scalars], *held)


def on_device_0(out_grad, out_weight, conv_input, gate_values, conv_output, filters, filter_reach):
    shape = jax.ShapeDtypeStruct
    rows, tok = conv_input.shape
    feats = out_grad.shape[1]
    seq_count = lax.axis_size("seq")
    place = lax.axis_index("seq").astype(jnp.int32)
    chan = lax.axis_index("chan").astype(jnp.int32)
    pos = jnp.stack([chan >> 1, chan & 1, place >> 3, (place >> 1) & 3, place])
    half = rows // 2
    scale = 1.0 / float(tok * seq_count) ** 0.5

    mine, other = call(
        gate_rows,
        [shape((half, tok), BF16)] * 2,
        (pos, conv_output, gate_values),
        scratch=[pltpu.VMEM((rows, tok), BF16)] * 2 + [pltpu.SemaphoreType.DMA((2,))],
        held_in=pltpu.HBM,
    )
    own = jnp.concatenate([mine, swap(other, "seq", 1)], axis=1)
    og_core = swap(out_grad, "seq", 1)
    pair = jnp.stack([own, swap(own, "chan", 1)])
    b1 = swap(pair, "chan", 2)
    b3 = swap(pair, "chan", 6)
    b2 = swap(pair, "chan", 4)

    keep, send = call(
        first_product,
        [shape((rows * 4, tok), BF16)] * 2,
        (pos, out_weight, out_grad),
        scratch=[
            pltpu.VMEM((4, 2 * rows, feats), BF16),
            pltpu.VMEM((tok, feats), BF16),
            pltpu.SemaphoreType.DMA((9,)),
        ],
        held_in=pltpu.HBM,
    )
    keep, s1, s3, s2 = call(
        middle_sums,
        [shape((rows, tok), F32)] + [shape((rows, tok), BF16)] * 3,
        (keep, swap(send, "chan", 1)),
        scalars=0,
    )
    s1, s3, s2 = swap(s1, "chan", 2), swap(s3, "chan", 6), swap(s2, "chan", 4)
    grad_gate, grad_conv = call(
        gate_grads,
        [shape((rows, tok), F32), shape((rows, tok), BF16)],
        (keep, s1, s3, s2, conv_output, gate_values),
        scalars=0,
    )

    halo_core = swap(grad_conv, "seq", 1)
    pairs = [(i, i + 1) for i in range(1, seq_count - 1, 2)]
    halo_out = lax.ppermute(grad_conv, "seq", pairs + [(b, a) for a, b in pairs])

    e = call(
        second_product,
        [shape((2, half, feats), BF16)] * 4,
        (pos, pair, b1, b3, b2, out_grad, og_core),
        scratch=[pltpu.VMEM((8, half, 2 * tok), BF16)],
    )
    e = [e[0], swap(e[1], "seq", 2), swap(e[2], "seq", 6), swap(e[3], "seq", 4)]

    groups = rows // 8
    tap_rows, input_rows = call(
        prepare,
        [
            shape((groups, 2, 128, 256), BF16),
            shape((groups, 2, 128, 2 * tok), BF16),
        ],
        (pos, filter_reach, filters, conv_input),
        scalars=2,
    )
    shifted = pltpu.VMEM((2, 256, 2 * tok), BF16)
    sums = pltpu.VMEM((seq_count, groups, 256), F32)
    grad_input, tap_sums = call(
        inner_side,
        [shape((rows, tok), F32), shape((seq_count, groups, 256), BF16)],
        (pos, grad_conv, halo_core, tap_rows, input_rows),
        scratch=[shifted, sums],
    )
    tap_sums = call(
        outer_taps,
        shape((seq_count, 2 * groups, 256), BF16),
        (pos, grad_conv, halo_out, input_rows, tap_sums),
        scratch=[shifted, sums],
    )
    tap_sums = lax.all_to_all(tap_sums, "seq", 0, 0)
    grad_input = call(
        outer_input,
        shape((rows, tok), F32),
        (pos, grad_conv, halo_out, tap_rows, grad_input),
        scratch=[shifted],
    )
    e_keep, e_send = call(
        sum_pieces, [shape((half, feats), F32), shape((half, feats), BF16)], e, scalars=0
    )
    e_got = swap(e_send, "seq", 8)
    grad_weight = call(
        functools.partial(finish_rows, scale=scale),
        shape((half, feats), F32),
        (e_keep, e_got),
        scalars=0,
    )
    grad_filters = call(
        functools.partial(finish_taps, scale=scale),
        shape((2, VN, rows), F32),
        (pos, filter_reach, tap_sums),
        scalars=2,
    )
    return (grad_input, grad_gate, grad_weight, jnp.transpose(grad_filters, (0, 2, 1)))


def solution(mesh):
    return jax.shard_map(
        on_device_0,
        mesh=mesh,
        in_specs=(
            P("seq", "chan"),
            P(None, "chan"),
            P("chan", "seq"),
            P("chan", "seq"),
            P("chan", "seq"),
            P(None, "chan", None),
            P(),
        ),
        out_specs=(P("chan", "seq"), P("chan", "seq"), P("seq", "chan"), P(None, "chan", "seq")),
        check_vma=False,
    )
```

```python
import functools

import jax
import jax.numpy as jnp
from jax import lax
from jax.experimental import pallas as pl
from jax.experimental.pallas import tpu as pltpu
from jax.sharding import PartitionSpec as P


GROUP = 64
VN = 32
F32 = jnp.float32
BF16 = jnp.bfloat16


def iota(shape, dim):
    return lax.broadcasted_iota(jnp.int32, shape, dim)


def dot(a, b, dims=(((1,), (0,)), ((), ()))):
    return lax.dot_general(a, b, dims, preferred_element_type=F32)


NT = (((1,), (1,)), ((), ()))


RELS = (0, 1, 3, 2)


def gate_rows(pos_ref, v_hbm, g_hbm, mine, other, v_ref, g_ref, sems):
    loads = [
        pltpu.make_async_copy(v_hbm, v_ref, sems.at[0]),
        pltpu.make_async_copy(g_hbm, g_ref, sems.at[1]),
    ]
    for load in loads:
        load.start()
    for load in loads:
        load.wait()
    half = mine.shape[0]
    core = pos_ref[4] & 1
    for ref, part in ((mine, core), (other, 1 - core)):
        band = pl.ds(pl.multiple_of(part * half, half), half)
        ref[...] = (v_ref[band, :].astype(F32) * g_ref[band, :].astype(F32)).astype(BF16)


def first_product(pos_ref, w_hbm, og_hbm, keep, send, w_ref, og_ref, sems):
    z = pos_ref[0]
    x = pos_ref[1]
    og_load = pltpu.make_async_copy(og_hbm, og_ref, sems.at[8])
    og_load.start()
    loads = []
    for i, rel in enumerate(RELS):
        for a in range(2):
            rows = pl.ds(pl.multiple_of(((z ^ rel) * 2 + (x ^ a)) * 128, 128), 128)
            part = w_ref.at[i, 128 * a : 128 * (a + 1)]
            loads.append(pltpu.make_async_copy(w_hbm.at[rows], part, sems.at[2 * i + a]))
            loads[-1].start()
    og_load.wait()
    og = og_ref[...]
    for i in range(4):
        loads[2 * i].wait()
        loads[2 * i + 1].wait()
        p = dot(w_ref[i], og, NT).astype(BF16)
        keep[128 * i : 128 * (i + 1), :] = p[:128]
        send[128 * i : 128 * (i + 1), :] = p[128:]


def middle_sums(k_ref, r_ref, *outs):
    n = k_ref.shape[0] // 4
    for i, ref in enumerate(outs):
        band = slice(n * i, n * i + n)
        ref[...] = (k_ref[band, :].astype(F32) + r_ref[band, :].astype(F32)).astype(ref.dtype)


def gate_grads(k_ref, r1, r3, r2, v_ref, g_ref, gate_ref, conv_ref):
    total = k_ref[...] + r1[...].astype(F32) + r3[...].astype(F32) + r2[...].astype(F32)
    gate_ref[...] = total * v_ref[...].astype(F32)
    conv_ref[...] = (total * g_ref[...].astype(F32)).astype(BF16)


def second_product(pos_ref, b0, b1, b3, b2, og_ref, ogs_ref, *refs):
    outs, g_ref = refs[:4], refs[4]
    for i, ref in enumerate((b0, b1, b2, b3)):
        g_ref[i] = ref[0]
        g_ref[4 + i] = ref[1]
    z = pos_ref[0]
    x = pos_ref[1]
    xh = pos_ref[2]
    y = pos_ref[3]
    tok = og_ref.shape[0]
    for ref, rel in zip(outs, RELS):
        for a in range(2):
            j = (xh ^ a) * 4 + (y ^ rel)
            g = g_ref[((j % 2) ^ x) * 4 + ((j // 2) ^ z)]
            ref[a] = (dot(g[:, :tok], og_ref[...]) + dot(g[:, tok:], ogs_ref[...])).astype(BF16)


def lagged(x, shifts, width):
    pair = [pltpu.roll(x, s % width, 1) if s % width else x for s in shifts]
    return jnp.concatenate(pair, axis=0).astype(BF16)


def prepare(pos_ref, reach_ref, f_ref, x_ref, l_ref, ui_ref, uo_ref):
    rows, n = x_ref.shape
    width = 3 * n
    chan = pos_ref[0] * 2 + pos_ref[1]
    own_rows = (iota((128, 256), 0) & 7) == (iota((128, 256), 1) & 7)
    ef = (iota((128, 256), 0) == (iota((128, 256), 1) >> 3)).astype(BF16)
    eb = (iota((128, 256), 0) == (VN - 1) - (iota((128, 256), 1) >> 3)).astype(BF16)
    taps = f_ref.shape[2]
    lag = iota((8, taps), 1)

    def step(i, carry):
        base = pl.multiple_of(i * 16, 16)
        band = pl.ds(base, 16)
        own16 = x_ref[band, :].astype(F32)
        filt16 = [f_ref[d, band, :].astype(F32) for d in range(2)]
        inside = lag < reach_ref[(chan * rows + base) // GROUP]
        zero = jnp.zeros((8, n), F32)
        for h in range(2):
            group = 2 * i + h
            for d, e in ((0, ef), (1, eb)):
                f8 = jnp.where(inside, filt16[d][8 * h : 8 * h + 8], 0.0)
                rolled = [f8 if b == 0 else pltpu.roll(f8, taps - 32 * b, 1) for b in range(4)]
                cut = [rolled[u % 4][:, 128 * (u // 4) : 128 * (u // 4) + 128] for u in range(16)]
                spread = dot(jnp.concatenate(cut, axis=0).astype(BF16), e)
                l_ref[group, d] = jnp.where(own_rows, spread, 0.0).astype(BF16)
            own = jnp.concatenate([zero, own16[8 * h : 8 * h + 8], zero], axis=1)
            bases = (
                (lagged(own, (0, 32), width), lagged(own, (64, 96), width)),
                (lagged(own, (-32, -64), width), lagged(own, (-96, -128), width)),
            )
            for d in range(2):
                for k in range(8):
                    start = n - 128 * (k // 2) if d == 0 else 128 * (k // 2)
                    part = bases[d][k % 2][:, start : start + 2 * n]
                    inner, outer = (part[:, :n], part[:, n:]) if d == 0 else (part[:, n:], part[:, :n])
                    at = 128 * d + 16 * k
                    ui_ref[group, at : at + 16, :] = inner
                    uo_ref[group, at : at + 16, :] = outer
        return carry

    lax.fori_loop(0, rows // 16, step, 0)


def conv_grads(pos_ref, gm_ref, gs_ref, gp_ref, l_ref, ui_ref, uo_ref,
               o_ref, t_ref, h_ref, acc_ref):
    rows, n = gm_ref.shape
    width = 3 * n
    lanes = n // 128
    core0 = (pos_ref[4] & 1) == 0
    own_cols = iota((16, 8, 256), 1) == (iota((16, 8, 256), 2) & 7)

    def step(i, carry):
        band = pl.ds(pl.multiple_of(i * 16, 16), 16)
        gm = gm_ref[band, :].astype(F32)
        gs = gs_ref[band, :].astype(F32)
        gp = gp_ref[band, :].astype(F32)
        ext16 = jnp.concatenate([jnp.where(core0, gp, gs), gm, jnp.where(core0, gs, gp)], axis=1)
        outs = []
        for h in range(2):
            group = 2 * i + h
            ext = ext16[8 * h : 8 * h + 8]
            two = jnp.concatenate([ext, pltpu.roll(ext, width - 1, 1)], axis=0).astype(BF16)
            for k in range(VN // 2):
                moved = two if k == 0 else pltpu.roll(two, width - 2 * k, 1)
                h_ref[h, 16 * k : 16 * k + 16, :] = moved
            total = None
            for d in range(2):
                acc = [[None] * (lanes + (b > 0)) for b in range(4)]
                for j in range(lanes):
                    if d == 0:
                        lo, hi = (0, 64) if j == 0 else (64, 128) if j == lanes - 1 else (0, 128)
                    else:
                        lo, hi = (48, 128) if j == 0 else (0, 64) if j == lanes - 1 else (0, 128)
                    at = n * (1 - d) + 256 * j
                    p = dot(l_ref[group, d, lo:hi, :], h_ref[h, :, at : at + 256])
                    for u in range(lo // 8, hi // 8):
                        a, b = divmod(u + d, 4)
                        for c in range(2):
                            q = 2 * j + c
                            slot = q - a if d == 0 else q - (lanes - (b > 0)) + a
                            if 0 <= slot < len(acc[b]):
                                part = p[8 * u - lo : 8 * u - lo + 8, 128 * c : 128 * c + 128]
                                acc[b][slot] = part if acc[b][slot] is None else acc[b][slot] + part
                for b in range(4):
                    line = jnp.concatenate(acc[b], axis=1)
                    if b and d == 0:
                        line = pltpu.roll(line, n + 128 - 32 * b, 1)[:, :n]
                    elif b:
                        line = pltpu.roll(line, 32 * b, 1)[:, 128:]
                    total = line if total is None else total + line
            outs.append(total)
            inner = dot(ui_ref[group], h_ref[h, :, n : 2 * n], NT)
            for d in range(2):
                start = 2 * n * (1 - d)
                cross = inner[128 * d : 128 * d + 128] + dot(
                    uo_ref[group, 128 * d : 128 * d + 128, :], h_ref[h, :, start : start + n], NT
                )
                sums = jnp.sum(jnp.where(own_cols, cross.reshape(16, 8, 256), 0.0), axis=1)
                row = d * (rows // 8) + group
                for u in range(16):
                    acc_ref[u, pl.ds(row, 1), :] = sums[u : u + 1]
        o_ref[band, :] = jnp.concatenate(outs, axis=0)
        return carry

    lax.fori_loop(0, rows // 16, step, 0)
    t_ref[...] = acc_ref[...].astype(BF16)


def sum_pieces(k, r1, r3, r2, keep, send):
    for ref, i in ((keep, 0), (send, 1)):
        total = k[i].astype(F32)
        for r in (r1, r3, r2):
            total = total + r[i].astype(F32)
        ref[...] = total.astype(ref.dtype)


def finish_rows(keep, got, o_ref, *, scale):
    o_ref[...] = (keep[...] + got[...].astype(F32)) * scale


def finish_taps(pos_ref, reach_ref, got, t_ref, *, scale):
    f = got[0].astype(F32)
    for i in range(1, got.shape[0]):
        f = f + got[i].astype(F32)
    chan = pos_ref[0] * 2 + pos_ref[1]
    place = pos_ref[4]
    own_cols = iota((16, 8, 256), 1) == (iota((16, 8, 256), 2) & 7)
    first = chan * 128 // GROUP
    limit = jnp.where(iota((VN, 128), 1) < GROUP, reach_ref[first], reach_ref[first + 1])
    inside = place * VN + iota((VN, 128), 0) < limit
    for d in range(2):
        v = iota((VN, 256), 1) >> 3
        e = (iota((VN, 256), 0) == (v if d == 0 else (VN - 1) - v)).astype(BF16)
        part = f[16 * d : 16 * d + 16, :]
        spread = jnp.broadcast_to(part[:, None, :], (16, 8, 256))
        spread = jnp.where(own_cols, spread, 0.0).reshape(128, 256)
        high = spread.astype(BF16)
        low = (spread - high.astype(F32)).astype(BF16)
        t_ref[d] = jnp.where(inside, (dot(e, high, NT) + dot(e, low, NT)) * scale, 0.0)


def swap(v, axis, mask):
    return lax.ppermute(v, axis, [(i, i ^ mask) for i in range(lax.axis_size(axis))])


def smem():
    return pl.BlockSpec(memory_space=pltpu.SMEM)


def call(body, out_shape, args, scalars=1, scratch=(), limit=16, held_in=pltpu.VMEM):
    vmem = pl.BlockSpec(memory_space=pltpu.VMEM)
    where = pl.BlockSpec(memory_space=held_in)
    held = [pltpu.with_memory_space_constraint(a, held_in) for a in args[scalars:]]
    return pl.pallas_call(
        body,
        out_shape=out_shape,
        in_specs=[smem()] * scalars + [where] * len(held),
        out_specs=jax.tree.map(lambda _: vmem, out_shape),
        scratch_shapes=list(scratch),
        compiler_params=pltpu.CompilerParams(vmem_limit_bytes=limit << 20),
    )(*args[:scalars], *held)


def on_device_0(out_grad, out_weight, conv_input, gate_values, conv_output, filters, filter_reach):
    shape = jax.ShapeDtypeStruct
    rows, tok = conv_input.shape
    feats = out_grad.shape[1]
    seq_count = lax.axis_size("seq")
    place = lax.axis_index("seq").astype(jnp.int32)
    chan = lax.axis_index("chan").astype(jnp.int32)
    pos = jnp.stack([chan >> 1, chan & 1, place >> 3, (place >> 1) & 3, place])
    half = rows // 2
    scale = 1.0 / float(tok * seq_count) ** 0.5

    mine, other = call(
        gate_rows,
        [shape((half, tok), BF16)] * 2,
        (pos, conv_output, gate_values),
        scratch=[pltpu.VMEM((rows, tok), BF16)] * 2 + [pltpu.SemaphoreType.DMA((2,))],
        held_in=pltpu.HBM,
    )
    own = jnp.concatenate([mine, swap(other, "seq", 1)], axis=1)
    og_core = swap(out_grad, "seq", 1)
    pair = jnp.stack([own, swap(own, "chan", 1)])
    b1 = swap(pair, "chan", 2)
    b3 = swap(pair, "chan", 6)
    b2 = swap(pair, "chan", 4)

    keep, send = call(
        first_product,
        [shape((rows * 4, tok), BF16)] * 2,
        (pos, out_weight, out_grad),
        scratch=[
            pltpu.VMEM((4, 2 * rows, feats), BF16),
            pltpu.VMEM((tok, feats), BF16),
            pltpu.SemaphoreType.DMA((9,)),
        ],
        held_in=pltpu.HBM,
    )
    keep, s1, s3, s2 = call(
        middle_sums,
        [shape((rows, tok), F32)] + [shape((rows, tok), BF16)] * 3,
        (keep, swap(send, "chan", 1)),
        scalars=0,
    )
    s1, s3, s2 = swap(s1, "chan", 2), swap(s3, "chan", 6), swap(s2, "chan", 4)
    grad_gate, grad_conv = call(
        gate_grads,
        [shape((rows, tok), F32), shape((rows, tok), BF16)],
        (keep, s1, s3, s2, conv_output, gate_values),
        scalars=0,
    )

    halo_core = swap(grad_conv, "seq", 1)
    pairs = [(i, i + 1) for i in range(1, seq_count - 1, 2)]
    halo_out = lax.ppermute(grad_conv, "seq", pairs + [(b, a) for a, b in pairs])

    e = call(
        second_product,
        [shape((2, half, feats), BF16)] * 4,
        (pos, pair, b1, b3, b2, out_grad, og_core),
        scratch=[pltpu.VMEM((8, half, 2 * tok), BF16)],
    )
    e = [e[0], swap(e[1], "seq", 2), swap(e[2], "seq", 6), swap(e[3], "seq", 4)]

    groups = rows // 8
    prepared = call(
        prepare,
        [
            shape((groups, 2, 128, 256), BF16),
            shape((groups, 256, tok), BF16),
            shape((groups, 256, tok), BF16),
        ],
        (pos, filter_reach, filters, conv_input),
        scalars=2,
    )
    grad_input, tap_sums = call(
        conv_grads,
        [shape((rows, tok), F32), shape((seq_count, rows // 4, 256), BF16)],
        (pos, grad_conv, halo_core, halo_out, *prepared),
        scratch=[
            pltpu.VMEM((2, 256, 3 * tok), BF16),
            pltpu.VMEM((seq_count, rows // 4, 256), F32),
        ],
    )
    tap_sums = lax.all_to_all(tap_sums, "seq", 0, 0)
    e_keep, e_send = call(
        sum_pieces, [shape((half, feats), F32), shape((half, feats), BF16)], e, scalars=0
    )
    e_got = swap(e_send, "seq", 8)
    grad_weight = call(
        functools.partial(finish_rows, scale=scale),
        shape((half, feats), F32),
        (e_keep, e_got),
        scalars=0,
    )
    grad_filters = call(
        functools.partial(finish_taps, scale=scale),
        shape((2, VN, rows), F32),
        (pos, filter_reach, tap_sums),
        scalars=2,
    )
    return (grad_input, grad_gate, grad_weight, jnp.transpose(grad_filters, (0, 2, 1)))


def solution(mesh):
    return jax.shard_map(
        on_device_0,
        mesh=mesh,
        in_specs=(
            P("seq", "chan"),
            P(None, "chan"),
            P("chan", "seq"),
            P("chan", "seq"),
            P("chan", "seq"),
            P(None, "chan", None),
            P(),
        ),
        out_specs=(P("chan", "seq"), P("chan", "seq"), P("seq", "chan"), P(None, "chan", "seq")),
        check_vma=False,
    )
```

```python
import functools

import jax
import jax.numpy as jnp
from jax import lax
from jax.experimental import pallas as pl
from jax.experimental.pallas import tpu as pltpu
from jax.sharding import PartitionSpec as P


GROUP = 64
VN = 32
JOINT = 8
F32 = jnp.float32
BF16 = jnp.bfloat16


def iota(shape, dim):
    return lax.broadcasted_iota(jnp.int32, shape, dim)


def dot(a, b, dims=(((1,), (0,)), ((), ()))):
    return lax.dot_general(a, b, dims, preferred_element_type=F32)


NT = (((1,), (1,)), ((), ()))


RELS = (0, 1, 3, 2)


def gate_rows(pos_ref, v_hbm, g_hbm, mine, other, v_ref, g_ref, sems):
    loads = [
        pltpu.make_async_copy(v_hbm, v_ref, sems.at[0]),
        pltpu.make_async_copy(g_hbm, g_ref, sems.at[1]),
    ]
    for load in loads:
        load.start()
    for load in loads:
        load.wait()
    half = mine.shape[0]
    core = pos_ref[4] & 1
    for ref, part in ((mine, core), (other, 1 - core)):
        band = pl.ds(pl.multiple_of(part * half, half), half)
        ref[...] = (v_ref[band, :].astype(F32) * g_ref[band, :].astype(F32)).astype(BF16)


def first_product(pos_ref, w_hbm, og_hbm, keep, send, w_ref, og_ref, sems):
    z = pos_ref[0]
    x = pos_ref[1]
    og_load = pltpu.make_async_copy(og_hbm, og_ref, sems.at[8])
    og_load.start()
    loads = []
    for i, rel in enumerate(RELS):
        for a in range(2):
            rows = pl.ds(pl.multiple_of(((z ^ rel) * 2 + (x ^ a)) * 128, 128), 128)
            part = w_ref.at[i, 128 * a : 128 * (a + 1)]
            loads.append(pltpu.make_async_copy(w_hbm.at[rows], part, sems.at[2 * i + a]))
            loads[-1].start()
    og_load.wait()
    og = og_ref[...]
    for i in range(4):
        loads[2 * i].wait()
        loads[2 * i + 1].wait()
        p = dot(w_ref[i], og, NT).astype(BF16)
        keep[128 * i : 128 * (i + 1), :] = p[:128]
        send[128 * i : 128 * (i + 1), :] = p[128:]


def middle_sums(k_ref, r_ref, *outs):
    n = k_ref.shape[0] // 4
    for i, ref in enumerate(outs):
        band = slice(n * i, n * i + n)
        ref[...] = (k_ref[band, :].astype(F32) + r_ref[band, :].astype(F32)).astype(ref.dtype)


def gate_grads(k_ref, r1, r3, r2, v_ref, g_ref, gate_ref, conv_ref):
    total = k_ref[...] + r1[...].astype(F32) + r3[...].astype(F32) + r2[...].astype(F32)
    gate_ref[...] = total * v_ref[...].astype(F32)
    conv_ref[...] = (total * g_ref[...].astype(F32)).astype(BF16)


def second_product(pos_ref, b0, b1, b3, b2, og_ref, ogs_ref, *refs):
    outs, g_ref = refs[:4], refs[4]
    for i, ref in enumerate((b0, b1, b2, b3)):
        g_ref[i] = ref[0]
        g_ref[4 + i] = ref[1]
    z = pos_ref[0]
    x = pos_ref[1]
    xh = pos_ref[2]
    y = pos_ref[3]
    tok = og_ref.shape[0]
    for ref, rel in zip(outs, RELS):
        for a in range(2):
            j = (xh ^ a) * 4 + (y ^ rel)
            g = g_ref[((j % 2) ^ x) * 4 + ((j // 2) ^ z)]
            ref[a] = (dot(g[:, :tok], og_ref[...]) + dot(g[:, tok:], ogs_ref[...])).astype(BF16)


def lagged(x, shifts, width):
    pair = [pltpu.roll(x, s % width, 1) if s % width else x for s in shifts]
    return jnp.concatenate(pair, axis=0).astype(BF16)


def prepare(pos_ref, reach_ref, f_ref, x_ref, l_ref, ui_ref, uo_ref):
    rows, n = x_ref.shape
    width = 3 * n
    chan = pos_ref[0] * 2 + pos_ref[1]
    own_rows = (iota((128, 256), 0) & 7) == (iota((128, 256), 1) & 7)
    ef = (iota((128, 256), 0) == (iota((128, 256), 1) >> 3)).astype(BF16)
    eb = (iota((128, 256), 0) == (VN - 1) - (iota((128, 256), 1) >> 3)).astype(BF16)
    taps = f_ref.shape[2]
    lag = iota((8, taps), 1)

    def step(i, carry):
        base = pl.multiple_of(i * 16, 16)
        band = pl.ds(base, 16)
        own16 = x_ref[band, :].astype(F32)
        filt16 = [f_ref[d, band, :].astype(F32) for d in range(2)]
        inside = lag < reach_ref[(chan * rows + base) // GROUP]
        zero = jnp.zeros((8, n), F32)
        for h in range(2):
            group = 2 * i + h
            for d, e in ((0, ef), (1, eb)):
                f8 = jnp.where(inside, filt16[d][8 * h : 8 * h + 8], 0.0)
                rolled = [f8 if b == 0 else pltpu.roll(f8, taps - 32 * b, 1) for b in range(4)]
                cut = [rolled[u % 4][:, 128 * (u // 4) : 128 * (u // 4) + 128] for u in range(16)]
                spread = dot(jnp.concatenate(cut, axis=0).astype(BF16), e)
                l_ref[group, d] = jnp.where(own_rows, spread, 0.0).astype(BF16)
            own = jnp.concatenate([zero, own16[8 * h : 8 * h + 8], zero], axis=1)
            bases = (
                (lagged(own, (0, 32), width), lagged(own, (64, 96), width)),
                (lagged(own, (-32, -64), width), lagged(own, (-96, -128), width)),
            )
            for d in range(2):
                for k in range(8):
                    start = n - 128 * (k // 2) if d == 0 else 128 * (k // 2)
                    part = bases[d][k % 2][:, start : start + 2 * n]
                    inner, outer = (part[:, :n], part[:, n:]) if d == 0 else (part[:, n:], part[:, :n])
                    at = 128 * d + 16 * k
                    ui_ref[group, at : at + 16, :] = inner
                    uo_ref[group, at : at + 16, :] = outer
        return carry

    lax.fori_loop(0, rows // 16, step, 0)


def conv_grads(pos_ref, gm_ref, gs_ref, gp_ref, l_ref, ui_ref, uo_ref,
               o_ref, keep_ref, send_ref, h_ref, t_ref):
    rows, n = gm_ref.shape
    width = 3 * n
    lanes = n // 128
    place = pos_ref[4]
    core0 = (place & 1) == 0
    own_cols = iota((16, 8, 256), 1) == (iota((16, 8, 256), 2) & 7)

    def step(i, carry):
        band = pl.ds(pl.multiple_of(i * 8 * JOINT, 8 * JOINT), 8 * JOINT)
        gm = gm_ref[band, :].astype(F32)
        gs = gs_ref[band, :].astype(F32)
        gp = gp_ref[band, :].astype(F32)
        ext16 = jnp.concatenate([jnp.where(core0, gp, gs), gm, jnp.where(core0, gs, gp)], axis=1)
        outs = []
        for h in range(JOINT):
            group = JOINT * i + h
            ext = ext16[8 * h : 8 * h + 8]
            two = jnp.concatenate([ext, pltpu.roll(ext, width - 1, 1)], axis=0).astype(BF16)
            for k in range(VN // 2):
                moved = two if k == 0 else pltpu.roll(two, width - 2 * k, 1)
                h_ref[h, 16 * k : 16 * k + 16, :] = moved
            total = None
            for d in range(2):
                acc = [[None] * (lanes + (b > 0)) for b in range(4)]
                for j in range(lanes):
                    if d == 0:
                        lo, hi = (0, 64) if j == 0 else (64, 128) if j == lanes - 1 else (0, 128)
                    else:
                        lo, hi = (48, 128) if j == 0 else (0, 64) if j == lanes - 1 else (0, 128)
                    at = n * (1 - d) + 256 * j
                    p = dot(l_ref[group, d, lo:hi, :], h_ref[h, :, at : at + 256])
                    for u in range(lo // 8, hi // 8):
                        a, b = divmod(u + d, 4)
                        for c in range(2):
                            q = 2 * j + c
                            slot = q - a if d == 0 else q - (lanes - (b > 0)) + a
                            if 0 <= slot < len(acc[b]):
                                part = p[8 * u - lo : 8 * u - lo + 8, 128 * c : 128 * c + 128]
                                acc[b][slot] = part if acc[b][slot] is None else acc[b][slot] + part
                for b in range(4):
                    line = jnp.concatenate(acc[b], axis=1)
                    if b and d == 0:
                        line = pltpu.roll(line, n + 128 - 32 * b, 1)[:, :n]
                    elif b:
                        line = pltpu.roll(line, 32 * b, 1)[:, 128:]
                    total = line if total is None else total + line
            outs.append(total)
            inner = dot(ui_ref[group], h_ref[h, :, n : 2 * n], NT)
            for d in range(2):
                start = 2 * n * (1 - d)
                cross = inner[128 * d : 128 * d + 128] + dot(
                    uo_ref[group, 128 * d : 128 * d + 128, :], h_ref[h, :, start : start + n], NT
                )
                sums = jnp.sum(jnp.where(own_cols, cross.reshape(16, 8, 256), 0.0), axis=1)
                row = d * (rows // 8) + group
                for u in range(16):
                    r = u ^ place
                    slot = (r & 1) * 8 + ((r >> 1) & 3) * 2 + (r >> 3)
                    t_ref[slot, pl.ds(row, 1), :] = sums[u : u + 1]
        o_ref[band, :] = jnp.concatenate(outs, axis=0)
        return carry

    lax.fori_loop(0, rows // (8 * JOINT), step, 0)
    keep_ref[...] = t_ref[0:8]
    send_ref[...] = t_ref[8:16].astype(BF16)


def split_taps(t_ref, got_ref, k, s1, s3, s2):
    for rel, ref in ((0, k), (1, s1), (3, s3), (2, s2)):
        both = t_ref[2 * rel : 2 * rel + 2] + got_ref[2 * rel : 2 * rel + 2].astype(F32)
        ref[...] = both.astype(ref.dtype)


def sum_pieces(k, r1, r3, r2, keep, send):
    for ref, i in ((keep, 0), (send, 1)):
        total = k[i].astype(F32)
        for r in (r1, r3, r2):
            total = total + r[i].astype(F32)
        ref[...] = total.astype(ref.dtype)


def finish_rows(keep, got, o_ref, *, scale):
    o_ref[...] = (keep[...] + got[...].astype(F32)) * scale


def finish_taps(pos_ref, reach_ref, part_ref, got, t_ref, *, scale):
    f = part_ref[...] + got[...].astype(F32)
    chan = pos_ref[0] * 2 + pos_ref[1]
    place = pos_ref[4]
    own_cols = iota((16, 8, 256), 1) == (iota((16, 8, 256), 2) & 7)
    first = chan * 128 // GROUP
    limit = jnp.where(iota((VN, 128), 1) < GROUP, reach_ref[first], reach_ref[first + 1])
    inside = place * VN + iota((VN, 128), 0) < limit
    for d in range(2):
        v = iota((VN, 256), 1) >> 3
        e = (iota((VN, 256), 0) == (v if d == 0 else (VN - 1) - v)).astype(BF16)
        part = f[16 * d : 16 * d + 16, :]
        spread = jnp.broadcast_to(part[:, None, :], (16, 8, 256))
        spread = jnp.where(own_cols, spread, 0.0).reshape(128, 256)
        high = spread.astype(BF16)
        low = (spread - high.astype(F32)).astype(BF16)
        t_ref[d] = jnp.where(inside, (dot(e, high, NT) + dot(e, low, NT)) * scale, 0.0)


def swap(v, axis, mask):
    return lax.ppermute(v, axis, [(i, i ^ mask) for i in range(lax.axis_size(axis))])


def smem():
    return pl.BlockSpec(memory_space=pltpu.SMEM)


def call(body, out_shape, args, scalars=1, scratch=(), limit=16, held_in=pltpu.VMEM):
    vmem = pl.BlockSpec(memory_space=pltpu.VMEM)
    where = pl.BlockSpec(memory_space=held_in)
    held = [pltpu.with_memory_space_constraint(a, held_in) for a in args[scalars:]]
    return pl.pallas_call(
        body,
        out_shape=out_shape,
        in_specs=[smem()] * scalars + [where] * len(held),
        out_specs=jax.tree.map(lambda _: vmem, out_shape),
        scratch_shapes=list(scratch),
        compiler_params=pltpu.CompilerParams(vmem_limit_bytes=limit << 20),
    )(*args[:scalars], *held)


def on_device_0(out_grad, out_weight, conv_input, gate_values, conv_output, filters, filter_reach):
    shape = jax.ShapeDtypeStruct
    rows, tok = conv_input.shape
    feats = out_grad.shape[1]
    seq_count = lax.axis_size("seq")
    place = lax.axis_index("seq").astype(jnp.int32)
    chan = lax.axis_index("chan").astype(jnp.int32)
    pos = jnp.stack([chan >> 1, chan & 1, place >> 3, (place >> 1) & 3, place])
    half = rows // 2
    scale = 1.0 / float(tok * seq_count) ** 0.5

    mine, other = call(
        gate_rows,
        [shape((half, tok), BF16)] * 2,
        (pos, conv_output, gate_values),
        scratch=[pltpu.VMEM((rows, tok), BF16)] * 2 + [pltpu.SemaphoreType.DMA((2,))],
        held_in=pltpu.HBM,
    )
    own = jnp.concatenate([mine, swap(other, "seq", 1)], axis=1)
    og_core = swap(out_grad, "seq", 1)
    pair = jnp.stack([own, swap(own, "chan", 1)])
    b1 = swap(pair, "chan", 2)
    b3 = swap(pair, "chan", 6)
    b2 = swap(pair, "chan", 4)

    keep, send = call(
        first_product,
        [shape((rows * 4, tok), BF16)] * 2,
        (pos, out_weight, out_grad),
        scratch=[
            pltpu.VMEM((4, 2 * rows, feats), BF16),
            pltpu.VMEM((tok, feats), BF16),
            pltpu.SemaphoreType.DMA((9,)),
        ],
        held_in=pltpu.HBM,
    )
    keep, s1, s3, s2 = call(
        middle_sums,
        [shape((rows, tok), F32)] + [shape((rows, tok), BF16)] * 3,
        (keep, swap(send, "chan", 1)),
        scalars=0,
    )
    s1, s3, s2 = swap(s1, "chan", 2), swap(s3, "chan", 6), swap(s2, "chan", 4)
    grad_gate, grad_conv = call(
        gate_grads,
        [shape((rows, tok), F32), shape((rows, tok), BF16)],
        (keep, s1, s3, s2, conv_output, gate_values),
        scalars=0,
    )

    halo_core = swap(grad_conv, "seq", 1)
    pairs = [(i, i + 1) for i in range(1, seq_count - 1, 2)]
    halo_out = lax.ppermute(grad_conv, "seq", pairs + [(b, a) for a, b in pairs])

    e = call(
        second_product,
        [shape((2, half, feats), BF16)] * 4,
        (pos, pair, b1, b3, b2, out_grad, og_core),
        scratch=[pltpu.VMEM((8, half, 2 * tok), BF16)],
    )
    e = [e[0], swap(e[1], "seq", 2), swap(e[2], "seq", 6), swap(e[3], "seq", 4)]

    groups = rows // 8
    prepared = call(
        prepare,
        [
            shape((groups, 2, 128, 256), BF16),
            shape((groups, 256, tok), BF16),
            shape((groups, 256, tok), BF16),
        ],
        (pos, filter_reach, filters, conv_input),
        scalars=2,
    )
    grad_input, tap_keep, tap_send = call(
        conv_grads,
        [
            shape((rows, tok), F32),
            shape((8, rows // 4, 256), F32),
            shape((8, rows // 4, 256), BF16),
        ],
        (pos, grad_conv, halo_core, halo_out, *prepared),
        scratch=[
            pltpu.VMEM((JOINT, 256, 3 * tok), BF16),
            pltpu.VMEM((16, rows // 4, 256), F32),
        ],
    )
    f_got = swap(tap_send, "seq", 1)
    piece = (2, rows // 4, 256)
    f = call(
        split_taps, [shape(piece, F32)] + [shape(piece, BF16)] * 3,
        (tap_keep, f_got), scalars=0,
    )
    f = [f[0], swap(f[1], "seq", 2), swap(f[2], "seq", 6), swap(f[3], "seq", 4)]
    e_keep, e_send = call(
        sum_pieces, [shape((half, feats), F32), shape((half, feats), BF16)], e, scalars=0
    )
    e_got = swap(e_send, "seq", 8)
    f_keep, f_send = call(sum_pieces, [shape(piece[1:], F32), shape(piece[1:], BF16)], f, scalars=0)
    f_got = swap(f_send, "seq", 8)
    grad_weight = call(
        functools.partial(finish_rows, scale=scale),
        shape((half, feats), F32),
        (e_keep, e_got),
        scalars=0,
    )
    grad_filters = call(
        functools.partial(finish_taps, scale=scale),
        shape((2, VN, rows), F32),
        (pos, filter_reach, f_keep, f_got),
        scalars=2,
    )
    return (grad_input, grad_gate, grad_weight, jnp.transpose(grad_filters, (0, 2, 1)))


def solution(mesh):
    return jax.shard_map(
        on_device_0,
        mesh=mesh,
        in_specs=(
            P("seq", "chan"),
            P(None, "chan"),
            P("chan", "seq"),
            P("chan", "seq"),
            P("chan", "seq"),
            P(None, "chan", None),
            P(),
        ),
        out_specs=(P("chan", "seq"), P("chan", "seq"), P("seq", "chan"), P(None, "chan", "seq")),
        check_vma=False,
    )
```

```python
import functools

import jax
import jax.numpy as jnp
from jax import lax
from jax.experimental import pallas as pl
from jax.experimental.pallas import tpu as pltpu
from jax.sharding import PartitionSpec as P


GROUP = 64
VN = 32
JOINT = 8
F32 = jnp.float32
BF16 = jnp.bfloat16


def iota(shape, dim):
    return lax.broadcasted_iota(jnp.int32, shape, dim)


def dot(a, b, dims=(((1,), (0,)), ((), ()))):
    return lax.dot_general(a, b, dims, preferred_element_type=F32)


NT = (((1,), (1,)), ((), ()))


RELS = (0, 1, 3, 2)


def gate_rows(pos_ref, v_hbm, g_hbm, mine, other, v_ref, g_ref, sems):
    loads = [
        pltpu.make_async_copy(v_hbm, v_ref, sems.at[0]),
        pltpu.make_async_copy(g_hbm, g_ref, sems.at[1]),
    ]
    for load in loads:
        load.start()
    for load in loads:
        load.wait()
    half = mine.shape[0]
    core = pos_ref[4] & 1
    for ref, part in ((mine, core), (other, 1 - core)):
        band = pl.ds(pl.multiple_of(part * half, half), half)
        ref[...] = (v_ref[band, :].astype(F32) * g_ref[band, :].astype(F32)).astype(BF16)


def first_product(pos_ref, w_hbm, og_hbm, keep, send, og_ref, w_ref, sems):
    z = pos_ref[0]
    x = pos_ref[1]
    og_load = pltpu.make_async_copy(og_hbm, og_ref, sems.at[8])
    og_load.start()
    loads = []
    for i, rel in enumerate(RELS):
        for a in range(2):
            rows = pl.ds(pl.multiple_of(((z ^ rel) * 2 + (x ^ a)) * 128, 128), 128)
            part = w_ref.at[i, 128 * a : 128 * (a + 1)]
            loads.append(pltpu.make_async_copy(w_hbm.at[rows], part, sems.at[2 * i + a]))
            loads[-1].start()
    og_load.wait()
    og = og_ref[...]
    for i in range(4):
        loads[2 * i].wait()
        loads[2 * i + 1].wait()
        p = dot(w_ref[i], og, NT).astype(BF16)
        keep[128 * i : 128 * (i + 1), :] = p[:128]
        send[128 * i : 128 * (i + 1), :] = p[128:]


def middle_sums(k_ref, r_ref, *outs):
    n = k_ref.shape[0] // 4
    for i, ref in enumerate(outs):
        band = slice(n * i, n * i + n)
        ref[...] = (k_ref[band, :].astype(F32) + r_ref[band, :].astype(F32)).astype(ref.dtype)


def gate_grads(k_ref, r1, r3, r2, g_ref, conv_ref, total_ref):
    total = k_ref[...] + r1[...].astype(F32) + r3[...].astype(F32) + r2[...].astype(F32)
    conv_ref[...] = (total * g_ref[...].astype(F32)).astype(BF16)
    total_ref[...] = total


def gate_output(total_ref, v_ref, gate_ref):
    gate_ref[...] = total_ref[...] * v_ref[...].astype(F32)


def second_product(pos_ref, b0, b1, b3, b2, og_ref, ogs_ref, *refs):
    outs, g_ref = refs[:4], refs[4]
    for i, ref in enumerate((b0, b1, b2, b3)):
        g_ref[i] = ref[0]
        g_ref[4 + i] = ref[1]
    z = pos_ref[0]
    x = pos_ref[1]
    xh = pos_ref[2]
    y = pos_ref[3]
    tok = og_ref.shape[0]
    for ref, rel in zip(outs, RELS):
        for a in range(2):
            j = (xh ^ a) * 4 + (y ^ rel)
            g = g_ref[((j % 2) ^ x) * 4 + ((j // 2) ^ z)]
            ref[a] = (dot(g[:, :tok], og_ref[...]) + dot(g[:, tok:], ogs_ref[...])).astype(BF16)


def lagged(x, shifts, width):
    pair = [pltpu.roll(x, s % width, 1) if s % width else x for s in shifts]
    return jnp.concatenate(pair, axis=0).astype(BF16)


def prepare(pos_ref, reach_ref, f_ref, x_ref, l_ref, ui_ref, uo_ref):
    rows, n = x_ref.shape
    width = 3 * n
    chan = pos_ref[0] * 2 + pos_ref[1]
    own_rows = (iota((128, 256), 0) & 7) == (iota((128, 256), 1) & 7)
    ef = (iota((128, 256), 0) == (iota((128, 256), 1) >> 3)).astype(BF16)
    eb = (iota((128, 256), 0) == (VN - 1) - (iota((128, 256), 1) >> 3)).astype(BF16)
    taps = f_ref.shape[2]
    lag = iota((8, taps), 1)

    def step(i, carry):
        base = pl.multiple_of(i * 16, 16)
        band = pl.ds(base, 16)
        own16 = x_ref[band, :].astype(F32)
        filt16 = [f_ref[d, band, :].astype(F32) for d in range(2)]
        inside = lag < reach_ref[(chan * rows + base) // GROUP]
        zero = jnp.zeros((8, n), F32)
        for h in range(2):
            group = 2 * i + h
            for d, e in ((0, ef), (1, eb)):
                f8 = jnp.where(inside, filt16[d][8 * h : 8 * h + 8], 0.0)
                rolled = [f8 if b == 0 else pltpu.roll(f8, taps - 32 * b, 1) for b in range(4)]
                cut = [rolled[u % 4][:, 128 * (u // 4) : 128 * (u // 4) + 128] for u in range(16)]
                spread = dot(jnp.concatenate(cut, axis=0).astype(BF16), e)
                l_ref[group, d] = jnp.where(own_rows, spread, 0.0).astype(BF16)
            own = jnp.concatenate([zero, own16[8 * h : 8 * h + 8], zero], axis=1)
            bases = (
                (lagged(own, (0, 32), width), lagged(own, (64, 96), width)),
                (lagged(own, (-32, -64), width), lagged(own, (-96, -128), width)),
            )
            for d in range(2):
                for k in range(8):
                    start = n - 128 * (k // 2) if d == 0 else 128 * (k // 2)
                    part = bases[d][k % 2][:, start : start + 2 * n]
                    inner, outer = (part[:, :n], part[:, n:]) if d == 0 else (part[:, n:], part[:, :n])
                    at = 128 * d + 16 * k
                    ui_ref[group, at : at + 16, :] = inner
                    uo_ref[group, at : at + 16, :] = outer
        return carry

    lax.fori_loop(0, rows // 16, step, 0)


def conv_grads(pos_ref, gm_ref, gs_ref, gp_ref, l_ref, ui_ref, uo_ref,
               o_ref, keep_ref, send_ref, h_ref, t_ref):
    rows, n = gm_ref.shape
    width = 3 * n
    lanes = n // 128
    place = pos_ref[4]
    core0 = (place & 1) == 0
    own_cols = iota((16, 8, 256), 1) == (iota((16, 8, 256), 2) & 7)

    def step(i, carry):
        band = pl.ds(pl.multiple_of(i * 8 * JOINT, 8 * JOINT), 8 * JOINT)
        gm = gm_ref[band, :].astype(F32)
        gs = gs_ref[band, :].astype(F32)
        gp = gp_ref[band, :].astype(F32)
        ext16 = jnp.concatenate([jnp.where(core0, gp, gs), gm, jnp.where(core0, gs, gp)], axis=1)
        outs = []
        for h in range(JOINT):
            group = JOINT * i + h
            ext = ext16[8 * h : 8 * h + 8]
            two = jnp.concatenate([ext, pltpu.roll(ext, width - 1, 1)], axis=0).astype(BF16)
            for k in range(VN // 2):
                moved = two if k == 0 else pltpu.roll(two, width - 2 * k, 1)
                h_ref[h, 16 * k : 16 * k + 16, :] = moved
            total = None
            for d in range(2):
                acc = [[None] * (lanes + (b > 0)) for b in range(4)]
                for j in range(lanes):
                    if d == 0:
                        lo, hi = (0, 64) if j == 0 else (64, 128) if j == lanes - 1 else (0, 128)
                    else:
                        lo, hi = (48, 128) if j == 0 else (0, 64) if j == lanes - 1 else (0, 128)
                    at = n * (1 - d) + 256 * j
                    p = dot(l_ref[group, d, lo:hi, :], h_ref[h, :, at : at + 256])
                    for u in range(lo // 8, hi // 8):
                        a, b = divmod(u + d, 4)
                        for c in range(2):
                            q = 2 * j + c
                            slot = q - a if d == 0 else q - (lanes - (b > 0)) + a
                            if 0 <= slot < len(acc[b]):
                                part = p[8 * u - lo : 8 * u - lo + 8, 128 * c : 128 * c + 128]
                                acc[b][slot] = part if acc[b][slot] is None else acc[b][slot] + part
                for b in range(4):
                    line = jnp.concatenate(acc[b], axis=1)
                    if b and d == 0:
                        line = pltpu.roll(line, n + 128 - 32 * b, 1)[:, :n]
                    elif b:
                        line = pltpu.roll(line, 32 * b, 1)[:, 128:]
                    total = line if total is None else total + line
            outs.append(total)
            inner = dot(ui_ref[group], h_ref[h, :, n : 2 * n], NT)
            for d in range(2):
                start = 2 * n * (1 - d)
                cross = inner[128 * d : 128 * d + 128] + dot(
                    uo_ref[group, 128 * d : 128 * d + 128, :], h_ref[h, :, start : start + n], NT
                )
                sums = jnp.sum(jnp.where(own_cols, cross.reshape(16, 8, 256), 0.0), axis=1)
                row = d * (rows // 8) + group
                for u in range(16):
                    r = u ^ place
                    slot = (r & 1) * 8 + ((r >> 1) & 3) * 2 + (r >> 3)
                    t_ref[slot, pl.ds(row, 1), :] = sums[u : u + 1]
        o_ref[band, :] = jnp.concatenate(outs, axis=0)
        return carry

    lax.fori_loop(0, rows // (8 * JOINT), step, 0)
    keep_ref[...] = t_ref[0:8]
    send_ref[...] = t_ref[8:16].astype(BF16)


def split_taps(t_ref, got_ref, k, s1, s3, s2):
    for rel, ref in ((0, k), (1, s1), (3, s3), (2, s2)):
        both = t_ref[2 * rel : 2 * rel + 2] + got_ref[2 * rel : 2 * rel + 2].astype(F32)
        ref[...] = both.astype(ref.dtype)


def sum_pieces(k, r1, r3, r2, keep, send):
    for ref, i in ((keep, 0), (send, 1)):
        total = k[i].astype(F32)
        for r in (r1, r3, r2):
            total = total + r[i].astype(F32)
        ref[...] = total.astype(ref.dtype)


def finish_rows(keep, got, o_ref, *, scale):
    o_ref[...] = (keep[...] + got[...].astype(F32)) * scale


def finish_taps(pos_ref, reach_ref, part_ref, got, t_ref, *, scale):
    f = part_ref[...] + got[...].astype(F32)
    chan = pos_ref[0] * 2 + pos_ref[1]
    place = pos_ref[4]
    own_cols = iota((16, 8, 256), 1) == (iota((16, 8, 256), 2) & 7)
    first = chan * 128 // GROUP
    limit = jnp.where(iota((VN, 128), 1) < GROUP, reach_ref[first], reach_ref[first + 1])
    inside = place * VN + iota((VN, 128), 0) < limit
    for d in range(2):
        v = iota((VN, 256), 1) >> 3
        e = (iota((VN, 256), 0) == (v if d == 0 else (VN - 1) - v)).astype(BF16)
        part = f[16 * d : 16 * d + 16, :]
        spread = jnp.broadcast_to(part[:, None, :], (16, 8, 256))
        spread = jnp.where(own_cols, spread, 0.0).reshape(128, 256)
        high = spread.astype(BF16)
        low = (spread - high.astype(F32)).astype(BF16)
        t_ref[d] = jnp.where(inside, (dot(e, high, NT) + dot(e, low, NT)) * scale, 0.0)


def swap(v, axis, mask):
    return lax.ppermute(v, axis, [(i, i ^ mask) for i in range(lax.axis_size(axis))])


def smem():
    return pl.BlockSpec(memory_space=pltpu.SMEM)


def call(body, out_shape, args, scalars=1, scratch=(), limit=16, held_in=pltpu.VMEM):
    vmem = pl.BlockSpec(memory_space=pltpu.VMEM)
    where = pl.BlockSpec(memory_space=held_in)
    held = [pltpu.with_memory_space_constraint(a, held_in) for a in args[scalars:]]
    return pl.pallas_call(
        body,
        out_shape=out_shape,
        in_specs=[smem()] * scalars + [where] * len(held),
        out_specs=jax.tree.map(lambda _: vmem, out_shape),
        scratch_shapes=list(scratch),
        compiler_params=pltpu.CompilerParams(vmem_limit_bytes=limit << 20),
    )(*args[:scalars], *held)


def on_device_0(out_grad, out_weight, conv_input, gate_values, conv_output, filters, filter_reach):
    shape = jax.ShapeDtypeStruct
    rows, tok = conv_input.shape
    feats = out_grad.shape[1]
    seq_count = lax.axis_size("seq")
    place = lax.axis_index("seq").astype(jnp.int32)
    chan = lax.axis_index("chan").astype(jnp.int32)
    pos = jnp.stack([chan >> 1, chan & 1, place >> 3, (place >> 1) & 3, place])
    half = rows // 2
    scale = 1.0 / float(tok * seq_count) ** 0.5

    mine, other = call(
        gate_rows,
        [shape((half, tok), BF16)] * 2,
        (pos, conv_output, gate_values),
        scratch=[pltpu.VMEM((rows, tok), BF16)] * 2 + [pltpu.SemaphoreType.DMA((2,))],
        held_in=pltpu.HBM,
    )
    own = jnp.concatenate([mine, swap(other, "seq", 1)], axis=1)
    og_core = swap(out_grad, "seq", 1)
    pair = jnp.stack([own, swap(own, "chan", 1)])
    b1 = swap(pair, "chan", 2)
    b3 = swap(pair, "chan", 6)
    b2 = swap(pair, "chan", 4)

    keep, send, og_local = call(
        first_product,
        [shape((rows * 4, tok), BF16)] * 2 + [shape((tok, feats), BF16)],
        (pos, out_weight, out_grad),
        scratch=[
            pltpu.VMEM((4, 2 * rows, feats), BF16),
            pltpu.SemaphoreType.DMA((9,)),
        ],
        held_in=pltpu.HBM,
    )
    keep, s1, s3, s2 = call(
        middle_sums,
        [shape((rows, tok), F32)] + [shape((rows, tok), BF16)] * 3,
        (keep, swap(send, "chan", 1)),
        scalars=0,
    )
    s1, s3, s2 = swap(s1, "chan", 2), swap(s3, "chan", 6), swap(s2, "chan", 4)
    grad_conv, total = call(
        gate_grads,
        [shape((rows, tok), BF16), shape((rows, tok), F32)],
        (keep, s1, s3, s2, gate_values),
        scalars=0,
    )
    grad_gate = call(gate_output, shape((rows, tok), F32), (total, conv_output), scalars=0)

    halo_core = swap(grad_conv, "seq", 1)
    pairs = [(i, i + 1) for i in range(1, seq_count - 1, 2)]
    halo_out = lax.ppermute(grad_conv, "seq", pairs + [(b, a) for a, b in pairs])

    e = call(
        second_product,
        [shape((2, half, feats), BF16)] * 4,
        (pos, pair, b1, b3, b2, og_local, og_core),
        scratch=[pltpu.VMEM((8, half, 2 * tok), BF16)],
    )
    e = [e[0], swap(e[1], "seq", 2), swap(e[2], "seq", 6), swap(e[3], "seq", 4)]

    groups = rows // 8
    prepared = call(
        prepare,
        [
            shape((groups, 2, 128, 256), BF16),
            shape((groups, 256, tok), BF16),
            shape((groups, 256, tok), BF16),
        ],
        (pos, filter_reach, filters, conv_input),
        scalars=2,
    )
    grad_input, tap_keep, tap_send = call(
        conv_grads,
        [
            shape((rows, tok), F32),
            shape((8, rows // 4, 256), F32),
            shape((8, rows // 4, 256), BF16),
        ],
        (pos, grad_conv, halo_core, halo_out, *prepared),
        scratch=[
            pltpu.VMEM((JOINT, 256, 3 * tok), BF16),
            pltpu.VMEM((16, rows // 4, 256), F32),
        ],
    )
    f_got = swap(tap_send, "seq", 1)
    piece = (2, rows // 4, 256)
    f = call(
        split_taps, [shape(piece, F32)] + [shape(piece, BF16)] * 3,
        (tap_keep, f_got), scalars=0,
    )
    f = [f[0], swap(f[1], "seq", 2), swap(f[2], "seq", 6), swap(f[3], "seq", 4)]
    e_keep, e_send = call(
        sum_pieces, [shape((half, feats), F32), shape((half, feats), BF16)], e, scalars=0
    )
    e_got = swap(e_send, "seq", 8)
    f_keep, f_send = call(sum_pieces, [shape(piece[1:], F32), shape(piece[1:], BF16)], f, scalars=0)
    f_got = swap(f_send, "seq", 8)
    grad_weight = call(
        functools.partial(finish_rows, scale=scale),
        shape((half, feats), F32),
        (e_keep, e_got),
        scalars=0,
    )
    grad_filters = call(
        functools.partial(finish_taps, scale=scale),
        shape((2, VN, rows), F32),
        (pos, filter_reach, f_keep, f_got),
        scalars=2,
    )
    return (grad_input, grad_gate, grad_weight, jnp.transpose(grad_filters, (0, 2, 1)))


def solution(mesh):
    return jax.shard_map(
        on_device_0,
        mesh=mesh,
        in_specs=(
            P("seq", "chan"),
            P(None, "chan"),
            P("chan", "seq"),
            P("chan", "seq"),
            P("chan", "seq"),
            P(None, "chan", None),
            P(),
        ),
        out_specs=(P("chan", "seq"), P("chan", "seq"), P("seq", "chan"), P(None, "chan", "seq")),
        check_vma=False,
    )
```

```python
import functools

import jax
import jax.numpy as jnp
from jax import lax
from jax.experimental import pallas as pl
from jax.experimental.pallas import tpu as pltpu
from jax.sharding import PartitionSpec as P


GROUP = 64
VN = 32
JOINT = 16
F32 = jnp.float32
BF16 = jnp.bfloat16


def iota(shape, dim):
    return lax.broadcasted_iota(jnp.int32, shape, dim)


def dot(a, b, dims=(((1,), (0,)), ((), ()))):
    return lax.dot_general(a, b, dims, preferred_element_type=F32)


NT = (((1,), (1,)), ((), ()))


RELS = (0, 1, 3, 2)


def gate_rows(pos_ref, v_hbm, g_hbm, w_hbm, og_hbm, mine, other, w_ref, og_ref, v_ref, g_ref, sems):
    z = pos_ref[0]
    x = pos_ref[1]
    loads = [(v_hbm, v_ref), (g_hbm, g_ref), (og_hbm, og_ref)]
    for i, rel in enumerate(RELS):
        for a in range(2):
            rows = pl.ds(pl.multiple_of(((z ^ rel) * 2 + (x ^ a)) * 128, 128), 128)
            loads.append((w_hbm.at[rows], w_ref.at[i, 128 * a : 128 * (a + 1)]))
    loads = [pltpu.make_async_copy(src, dst, sems.at[i]) for i, (src, dst) in enumerate(loads)]
    for load in loads:
        load.start()
    loads[0].wait()
    loads[1].wait()
    half = mine.shape[0]
    core = pos_ref[4] & 1
    for ref, part in ((mine, core), (other, 1 - core)):
        band = pl.ds(pl.multiple_of(part * half, half), half)
        ref[...] = (v_ref[band, :].astype(F32) * g_ref[band, :].astype(F32)).astype(BF16)
    for load in loads[2:]:
        load.wait()


def first_product(w_ref, og_ref, keep, send):
    og = og_ref[...]
    for i in range(4):
        p = dot(w_ref[i], og, NT).astype(BF16)
        keep[128 * i : 128 * (i + 1), :] = p[:128]
        send[128 * i : 128 * (i + 1), :] = p[128:]


def middle_sums(k_ref, r_ref, *outs):
    n = k_ref.shape[0] // 4
    for i, ref in enumerate(outs):
        band = slice(n * i, n * i + n)
        ref[...] = (k_ref[band, :].astype(F32) + r_ref[band, :].astype(F32)).astype(ref.dtype)


def gate_grads(k_ref, r1, r3, r2, g_ref, conv_ref, total_ref):
    total = k_ref[...] + r1[...].astype(F32) + r3[...].astype(F32) + r2[...].astype(F32)
    conv_ref[...] = (total * g_ref[...].astype(F32)).astype(BF16)
    total_ref[...] = total


def gate_output(total_ref, v_ref, gate_ref):
    gate_ref[...] = total_ref[...] * v_ref[...].astype(F32)


def second_product(pos_ref, b0, b1, b3, b2, og_ref, ogs_ref, *refs):
    outs, g_ref = refs[:4], refs[4]
    for i, ref in enumerate((b0, b1, b2, b3)):
        g_ref[i] = ref[0]
        g_ref[4 + i] = ref[1]
    z = pos_ref[0]
    x = pos_ref[1]
    xh = pos_ref[2]
    y = pos_ref[3]
    tok = og_ref.shape[0]
    for ref, rel in zip(outs, RELS):
        for a in range(2):
            j = (xh ^ a) * 4 + (y ^ rel)
            g = g_ref[((j % 2) ^ x) * 4 + ((j // 2) ^ z)]
            ref[a] = (dot(g[:, :tok], og_ref[...]) + dot(g[:, tok:], ogs_ref[...])).astype(BF16)


def lagged(x, shifts, width):
    pair = [pltpu.roll(x, s % width, 1) if s % width else x for s in shifts]
    return jnp.concatenate(pair, axis=0).astype(BF16)


def prepare(pos_ref, reach_ref, f_ref, x_ref, l_ref, ui_ref, uo_ref):
    rows, n = x_ref.shape
    width = 3 * n
    chan = pos_ref[0] * 2 + pos_ref[1]
    own_rows = (iota((128, 256), 0) & 7) == (iota((128, 256), 1) & 7)
    ef = (iota((128, 256), 0) == (iota((128, 256), 1) >> 3)).astype(BF16)
    eb = (iota((128, 256), 0) == (VN - 1) - (iota((128, 256), 1) >> 3)).astype(BF16)
    taps = f_ref.shape[2]
    lag = iota((8, taps), 1)

    def step(i, carry):
        base = pl.multiple_of(i * 16, 16)
        band = pl.ds(base, 16)
        own16 = x_ref[band, :].astype(F32)
        filt16 = [f_ref[d, band, :].astype(F32) for d in range(2)]
        inside = lag < reach_ref[(chan * rows + base) // GROUP]
        zero = jnp.zeros((8, n), F32)
        for h in range(2):
            group = 2 * i + h
            for d, e in ((0, ef), (1, eb)):
                f8 = jnp.where(inside, filt16[d][8 * h : 8 * h + 8], 0.0)
                rolled = [f8 if b == 0 else pltpu.roll(f8, taps - 32 * b, 1) for b in range(4)]
                cut = [rolled[u % 4][:, 128 * (u // 4) : 128 * (u // 4) + 128] for u in range(16)]
                spread = dot(jnp.concatenate(cut, axis=0).astype(BF16), e)
                l_ref[group, d] = jnp.where(own_rows, spread, 0.0).astype(BF16)
            own = jnp.concatenate([zero, own16[8 * h : 8 * h + 8], zero], axis=1)
            bases = (
                (lagged(own, (0, 32), width), lagged(own, (64, 96), width)),
                (lagged(own, (-32, -64), width), lagged(own, (-96, -128), width)),
            )
            for d in range(2):
                for k in range(8):
                    start = n - 128 * (k // 2) if d == 0 else 128 * (k // 2)
                    part = bases[d][k % 2][:, start : start + 2 * n]
                    inner, outer = (part[:, :n], part[:, n:]) if d == 0 else (part[:, n:], part[:, :n])
                    at = 128 * d + 16 * k
                    ui_ref[group, at : at + 16, :] = inner
                    uo_ref[group, at : at + 16, :] = outer
        return carry

    lax.fori_loop(0, rows // 16, step, 0)


def conv_grads(pos_ref, gm_ref, gs_ref, gp_ref, l_ref, ui_ref, uo_ref,
               o_ref, keep_ref, send_ref, h_ref, t_ref):
    rows, n = gm_ref.shape
    width = 3 * n
    lanes = n // 128
    place = pos_ref[4]
    core0 = (place & 1) == 0
    own_cols = iota((16, 8, 256), 1) == (iota((16, 8, 256), 2) & 7)

    def step(i, carry):
        band = pl.ds(pl.multiple_of(i * 8 * JOINT, 8 * JOINT), 8 * JOINT)
        gm = gm_ref[band, :].astype(F32)
        gs = gs_ref[band, :].astype(F32)
        gp = gp_ref[band, :].astype(F32)
        ext16 = jnp.concatenate([jnp.where(core0, gp, gs), gm, jnp.where(core0, gs, gp)], axis=1)
        outs = []
        for h in range(JOINT):
            group = JOINT * i + h
            ext = ext16[8 * h : 8 * h + 8]
            two = jnp.concatenate([ext, pltpu.roll(ext, width - 1, 1)], axis=0).astype(BF16)
            for k in range(VN // 2):
                moved = two if k == 0 else pltpu.roll(two, width - 2 * k, 1)
                h_ref[h, 16 * k : 16 * k + 16, :] = moved
            total = None
            for d in range(2):
                acc = [[None] * (lanes + (b > 0)) for b in range(4)]
                for j in range(lanes):
                    if d == 0:
                        lo, hi = (0, 64) if j == 0 else (64, 128) if j == lanes - 1 else (0, 128)
                    else:
                        lo, hi = (48, 128) if j == 0 else (0, 64) if j == lanes - 1 else (0, 128)
                    at = n * (1 - d) + 256 * j
                    p = dot(l_ref[group, d, lo:hi, :], h_ref[h, :, at : at + 256])
                    for u in range(lo // 8, hi // 8):
                        a, b = divmod(u + d, 4)
                        for c in range(2):
                            q = 2 * j + c
                            slot = q - a if d == 0 else q - (lanes - (b > 0)) + a
                            if 0 <= slot < len(acc[b]):
                                part = p[8 * u - lo : 8 * u - lo + 8, 128 * c : 128 * c + 128]
                                acc[b][slot] = part if acc[b][slot] is None else acc[b][slot] + part
                for b in range(4):
                    line = jnp.concatenate(acc[b], axis=1)
                    if b and d == 0:
                        line = pltpu.roll(line, n + 128 - 32 * b, 1)[:, :n]
                    elif b:
                        line = pltpu.roll(line, 32 * b, 1)[:, 128:]
                    total = line if total is None else total + line
            outs.append(total)
            inner = dot(ui_ref[group], h_ref[h, :, n : 2 * n], NT)
            for d in range(2):
                start = 2 * n * (1 - d)
                cross = inner[128 * d : 128 * d + 128] + dot(
                    uo_ref[group, 128 * d : 128 * d + 128, :], h_ref[h, :, start : start + n], NT
                )
                sums = jnp.sum(jnp.where(own_cols, cross.reshape(16, 8, 256), 0.0), axis=1)
                row = d * (rows // 8) + group
                for u in range(16):
                    r = u ^ place
                    slot = (r & 1) * 8 + ((r >> 1) & 3) * 2 + (r >> 3)
                    t_ref[slot, pl.ds(row, 1), :] = sums[u : u + 1]
        o_ref[band, :] = jnp.concatenate(outs, axis=0)
        return carry

    lax.fori_loop(0, rows // (8 * JOINT), step, 0)
    keep_ref[...] = t_ref[0:8]
    send_ref[...] = t_ref[8:16].astype(BF16)


def split_taps(t_ref, got_ref, k, s1, s3, s2):
    for rel, ref in ((0, k), (1, s1), (3, s3), (2, s2)):
        both = t_ref[2 * rel : 2 * rel + 2] + got_ref[2 * rel : 2 * rel + 2].astype(F32)
        ref[...] = both.astype(ref.dtype)


def sum_pieces(k, r1, r3, r2, keep, send):
    for ref, i in ((keep, 0), (send, 1)):
        total = k[i].astype(F32)
        for r in (r1, r3, r2):
            total = total + r[i].astype(F32)
        ref[...] = total.astype(ref.dtype)


def finish_rows(keep, got, o_ref, *, scale):
    o_ref[...] = (keep[...] + got[...].astype(F32)) * scale


def finish_taps(pos_ref, reach_ref, part_ref, got, t_ref, *, scale):
    f = part_ref[...] + got[...].astype(F32)
    chan = pos_ref[0] * 2 + pos_ref[1]
    place = pos_ref[4]
    own_cols = iota((16, 8, 256), 1) == (iota((16, 8, 256), 2) & 7)
    first = chan * 128 // GROUP
    limit = jnp.where(iota((VN, 128), 1) < GROUP, reach_ref[first], reach_ref[first + 1])
    inside = place * VN + iota((VN, 128), 0) < limit
    for d in range(2):
        v = iota((VN, 256), 1) >> 3
        e = (iota((VN, 256), 0) == (v if d == 0 else (VN - 1) - v)).astype(BF16)
        part = f[16 * d : 16 * d + 16, :]
        spread = jnp.broadcast_to(part[:, None, :], (16, 8, 256))
        spread = jnp.where(own_cols, spread, 0.0).reshape(128, 256)
        high = spread.astype(BF16)
        low = (spread - high.astype(F32)).astype(BF16)
        t_ref[d] = jnp.where(inside, (dot(e, high, NT) + dot(e, low, NT)) * scale, 0.0)


def swap(v, axis, mask):
    return lax.ppermute(v, axis, [(i, i ^ mask) for i in range(lax.axis_size(axis))])


def smem():
    return pl.BlockSpec(memory_space=pltpu.SMEM)


def call(body, out_shape, args, scalars=1, scratch=(), limit=16, held_in=pltpu.VMEM):
    vmem = pl.BlockSpec(memory_space=pltpu.VMEM)
    where = pl.BlockSpec(memory_space=held_in)
    held = [pltpu.with_memory_space_constraint(a, held_in) for a in args[scalars:]]
    return pl.pallas_call(
        body,
        out_shape=out_shape,
        in_specs=[smem()] * scalars + [where] * len(held),
        out_specs=jax.tree.map(lambda _: vmem, out_shape),
        scratch_shapes=list(scratch),
        compiler_params=pltpu.CompilerParams(vmem_limit_bytes=limit << 20),
    )(*args[:scalars], *held)


def on_device_0(out_grad, out_weight, conv_input, gate_values, conv_output, filters, filter_reach):
    shape = jax.ShapeDtypeStruct
    rows, tok = conv_input.shape
    feats = out_grad.shape[1]
    seq_count = lax.axis_size("seq")
    place = lax.axis_index("seq").astype(jnp.int32)
    chan = lax.axis_index("chan").astype(jnp.int32)
    pos = jnp.stack([chan >> 1, chan & 1, place >> 3, (place >> 1) & 3, place])
    half = rows // 2
    scale = 1.0 / float(tok * seq_count) ** 0.5

    mine, other, weight, grad_local = call(
        gate_rows,
        [shape((half, tok), BF16)] * 2
        + [shape((4, 2 * rows, feats), BF16), shape((tok, feats), BF16)],
        (pos, conv_output, gate_values, out_weight, out_grad),
        scratch=[pltpu.VMEM((rows, tok), BF16)] * 2 + [pltpu.SemaphoreType.DMA((11,))],
        held_in=pltpu.HBM,
    )
    own = jnp.concatenate([mine, swap(other, "seq", 1)], axis=1)
    og_core = swap(grad_local, "seq", 1)
    pair = jnp.stack([own, swap(own, "chan", 1)])
    b1 = swap(pair, "chan", 2)
    b3 = swap(pair, "chan", 6)
    b2 = swap(pair, "chan", 4)

    keep, send = call(
        first_product, [shape((rows * 4, tok), BF16)] * 2, (weight, grad_local), scalars=0
    )
    keep, s1, s3, s2 = call(
        middle_sums,
        [shape((rows, tok), F32)] + [shape((rows, tok), BF16)] * 3,
        (keep, swap(send, "chan", 1)),
        scalars=0,
    )
    s1, s3, s2 = swap(s1, "chan", 2), swap(s3, "chan", 6), swap(s2, "chan", 4)
    grad_conv, total = call(
        gate_grads,
        [shape((rows, tok), BF16), shape((rows, tok), F32)],
        (keep, s1, s3, s2, gate_values),
        scalars=0,
    )
    grad_gate = call(gate_output, shape((rows, tok), F32), (total, conv_output), scalars=0)

    halo_core = swap(grad_conv, "seq", 1)
    pairs = [(i, i + 1) for i in range(1, seq_count - 1, 2)]
    halo_out = lax.ppermute(grad_conv, "seq", pairs + [(b, a) for a, b in pairs])

    e = call(
        second_product,
        [shape((2, half, feats), BF16)] * 4,
        (pos, pair, b1, b3, b2, grad_local, og_core),
        scratch=[pltpu.VMEM((8, half, 2 * tok), BF16)],
    )
    e = [e[0], swap(e[1], "seq", 2), swap(e[2], "seq", 6), swap(e[3], "seq", 4)]

    groups = rows // 8
    prepared = call(
        prepare,
        [
            shape((groups, 2, 128, 256), BF16),
            shape((groups, 256, tok), BF16),
            shape((groups, 256, tok), BF16),
        ],
        (pos, filter_reach, filters, conv_input),
        scalars=2,
    )
    grad_input, tap_keep, tap_send = call(
        conv_grads,
        [
            shape((rows, tok), F32),
            shape((8, rows // 4, 256), F32),
            shape((8, rows // 4, 256), BF16),
        ],
        (pos, grad_conv, halo_core, halo_out, *prepared),
        scratch=[
            pltpu.VMEM((JOINT, 256, 3 * tok), BF16),
            pltpu.VMEM((16, rows // 4, 256), F32),
        ],
    )
    f_got = swap(tap_send, "seq", 1)
    piece = (2, rows // 4, 256)
    f = call(
        split_taps, [shape(piece, F32)] + [shape(piece, BF16)] * 3,
        (tap_keep, f_got), scalars=0,
    )
    f = [f[0], swap(f[1], "seq", 2), swap(f[2], "seq", 6), swap(f[3], "seq", 4)]
    e_keep, e_send = call(
        sum_pieces, [shape((half, feats), F32), shape((half, feats), BF16)], e, scalars=0
    )
    e_got = swap(e_send, "seq", 8)
    f_keep, f_send = call(sum_pieces, [shape(piece[1:], F32), shape(piece[1:], BF16)], f, scalars=0)
    f_got = swap(f_send, "seq", 8)
    grad_weight = call(
        functools.partial(finish_rows, scale=scale),
        shape((half, feats), F32),
        (e_keep, e_got),
        scalars=0,
    )
    grad_filters = call(
        functools.partial(finish_taps, scale=scale),
        shape((2, VN, rows), F32),
        (pos, filter_reach, f_keep, f_got),
        scalars=2,
    )
    return (grad_input, grad_gate, grad_weight, jnp.transpose(grad_filters, (0, 2, 1)))


def solution(mesh):
    return jax.shard_map(
        on_device_0,
        mesh=mesh,
        in_specs=(
            P("seq", "chan"),
            P(None, "chan"),
            P("chan", "seq"),
            P("chan", "seq"),
            P("chan", "seq"),
            P(None, "chan", None),
            P(),
        ),
        out_specs=(P("chan", "seq"), P("chan", "seq"), P("seq", "chan"), P(None, "chan", "seq")),
        check_vma=False,
    )
```
